32 devices in a mesh: ctx: 16 (over z, y, core), section: 2 (over x).
Axes of the slice: x: 2, y: 2, z: 4, core: 2. Of those that a mesh axis runs over, the one named last changes fastest.
Arguments:
- queries: bfloat16 [2, 2048, 2560], P('section', 'ctx'), may hold values from -80 to 80
- grad_out: bfloat16 [2, 2048, 2560], P('section', 'ctx'), may hold values from -6 to 6
- keys_values: bfloat16 [2, 2048, 512], P(None, 'ctx'), may hold values from -16 to 16
- doc_ids: int32 [2048], replicated, may hold values from 0 to 7, never falling along the last dimension, each value on 1 to 512 neighbouring positions
Outputs:
- grad_queries: bfloat16 [2, 2048, 2560], P('section', 'ctx')
- grad_kv: bfloat16 [2, 2048, 512], P(None, ('ctx', 'section'))
The draws below stay inside these ranges and needn't reach their ends.
Inputs may be any that keep to these rules, and one draw needn't show every extreme that they name: `doc_ids`: document numbers never fall along the sequence; a document has at most 512 tokens.
All inputs are finite; a program needn't handle non-finite values.
Results may differ from the reference program's by a relative error of at most 0.015.
Values may be sent and summed in bfloat16 or wider, within the bound.
A program may use at most 64 MiB of HBM per device.

```python
import math
import jax
import jax.numpy as jnp
import numpy as np
from jax import lax

HD = 128
KVH = 4
GROUP = 5
TOKENS = 2048
LAYERS = 2
HEADS = 20


def cache_base(key):
    keys = jnp.clip(jax.random.normal(jax.random.fold_in(key, 11), (TOKENS, KVH, HD), jnp.float32), -5.0, 5.0)
    values = jnp.clip(jax.random.normal(jax.random.fold_in(key, 12), (TOKENS, KVH, HD), jnp.float32), -5.0, 5.0)
    return (keys, values)


def draw_keys_values(key, part):
    keys, values = cache_base(key)
    return jnp.stack([keys, values]).reshape(2, TOKENS, KVH * HD).astype(jnp.bfloat16)


def draw_queries(key, part):
    shaped = jnp.clip(jax.random.normal(jax.random.fold_in(key, 13), (LAYERS, TOKENS, KVH, GROUP, HD), jnp.float32), -5.0, 5.0)
    return shaped.reshape(LAYERS, TOKENS, KVH * GROUP * HD).astype(jnp.bfloat16)


def level_of(stream_key, dims, cuts, smallest, top_value):
    loudness = 1.0
    for axis_at, shards_of in cuts:
        steps = jax.random.uniform(jax.random.fold_in(jax.random.fold_in(stream_key, 6), axis_at), (shards_of,), jnp.float32, smallest / len(cuts), top_value / len(cuts))
        loudness = loudness * jnp.repeat(jnp.exp(steps), dims[axis_at] // shards_of).reshape((-1,) + (1,) * (len(dims) - 1 - axis_at))
    return loudness


def split_up(number_of, total, reach, lean):
    portions = [(1 << 20) // math.isqrt(standing ** lean) + 1 for standing in range(2, number_of + 1)]
    spare, holding = total - reach - (number_of - 1), [1] * (number_of - 1)
    while spare > 0:
        free = [i for i in range(number_of - 1) if holding[i] < reach]
        mass, budget = sum([portions[i] for i in free]), spare
        for i in free:
            addition = min(reach - holding[i], max(1, budget * portions[i] // mass), spare)
            holding[i] = holding[i] + addition
            spare = spare - addition
    return np.array([reach] + holding)


def ragged_sizes(stream_key, amount, total, reach, lean):
    if amount == 2:
        one = jax.random.randint(stream_key, (), max(1, total - reach), min(reach, total - 1) + 1)
        return jnp.stack([one, total - one])
    lengths = jnp.asarray(split_up(amount, total, reach, lean), jnp.int32)
    twos = (amount - 1) // 2
    giver, receiver = lengths[1:1 + 2 * twos:2], lengths[2:2 + 2 * twos:2]
    room = jnp.minimum(giver - 1, reach - receiver)
    moved = jax.random.randint(jax.random.fold_in(stream_key, 1), (twos,), 0, 1 << 20) % (room + 1)
    lengths = lengths.at[1:1 + 2 * twos:2].set(giver - moved).at[2:2 + 2 * twos:2].set(receiver + moved)
    return lengths[jax.random.permutation(jax.random.fold_in(stream_key, 2), amount)]


def noise(own_key, dims, spread, limit, split=(), kind=jnp.bfloat16):
    result = jax.random.normal(own_key, dims, jnp.float32) * spread
    if len(split) > 0:
        result = level_of(own_key, dims, split, -0.22, 0.18) * result
    return jnp.clip(result, min=-limit, max=limit).astype(kind)


def setup_inputs(seed: int = 0) -> dict:
    streams_of = jax.random.split(jax.random.key(seed), 5)
    queries = draw_queries(jax.random.fold_in(streams_of[4], 71), 0)
    grad_out = noise(streams_of[1], (LAYERS, TOKENS, HEADS * HD), 1.0, 6.0, ((0, 2), (1, 16)))
    keys_values = draw_keys_values(jax.random.fold_in(streams_of[4], 71), 0)
    doc_ids = jnp.searchsorted(jnp.cumsum(ragged_sizes(streams_of[3], 8, TOKENS, TOKENS // 4, 1)), jnp.arange(TOKENS), side="right").astype(jnp.int32)
    return {"queries": queries, "grad_out": grad_out, "keys_values": keys_values, "doc_ids": doc_ids}


def reference(queries, grad_out, keys_values, doc_ids):
    scale = HD ** -0.5
    keys = keys_values[0].reshape(TOKENS, KVH, HD).astype(jnp.float32)
    values = keys_values[1].reshape(TOKENS, KVH, HD).astype(jnp.float32)
    qblock = min(512, TOKENS)
    nblocks = TOKENS // qblock
    places = jnp.arange(TOKENS, dtype=jnp.int32)

    def one_block(carry, index):
        layer = index // nblocks
        start = (index % nblocks) * qblock
        qrows = lax.dynamic_slice_in_dim(queries[layer], start, qblock, 0).reshape(qblock, KVH, GROUP, HD).astype(jnp.float32)
        grows = lax.dynamic_slice_in_dim(grad_out[layer], start, qblock, 0).reshape(qblock, KVH, GROUP, HD).astype(jnp.float32)
        qplace = start + jnp.arange(qblock, dtype=jnp.int32)
        qdoc = lax.dynamic_slice_in_dim(doc_ids, start, qblock, 0)
        visible = (places[None, :] <= qplace[:, None]) & (doc_ids[None, :] == qdoc[:, None])
        seen = visible[:, None, None, :]
        scores = jnp.einsum("rgnd,kgd->rgnk", qrows, keys) * scale
        scores = jnp.where(seen, scores, -1e30)
        top = jnp.max(scores, axis=-1)
        lse = top + jnp.log(jnp.sum(jnp.exp(scores - top[..., None]), axis=-1))
        weights = jnp.where(seen, jnp.exp(scores - lse[..., None]), 0.0)
        out = jnp.einsum("rgnk,kgd->rgnd", weights, values, precision=lax.Precision.HIGHEST)
        delta = jnp.sum(grows * out, axis=-1)
        prob = weights.astype(jnp.bfloat16).astype(jnp.float32)
        dprob = jnp.einsum("rgnd,kgd->rgnk", grows, values)
        dscore = (prob * (dprob - delta[..., None])).astype(jnp.bfloat16).astype(jnp.float32)
        dquery = (scale * jnp.einsum("rgnk,kgd->rgnd", dscore, keys)).astype(jnp.bfloat16)
        dkeys = scale * jnp.einsum("rgnk,rgnd->kgd", dscore, qrows)
        dvalues = jnp.einsum("rgnk,rgnd->kgd", prob, grows)
        return (carry[0] + dkeys, carry[1] + dvalues), dquery.reshape(qblock, HEADS * HD)

    start_sums = (jnp.zeros((TOKENS, KVH, HD), jnp.float32), jnp.zeros((TOKENS, KVH, HD), jnp.float32))
    sums, dqueries = lax.scan(one_block, start_sums, jnp.arange(LAYERS * nblocks, dtype=jnp.int32))
    grad_queries = dqueries.reshape(LAYERS, TOKENS, HEADS * HD)
    grad_kv = jnp.stack([sums[0], sums[1]]).reshape(2, TOKENS, KVH * HD).astype(jnp.bfloat16)
    return grad_queries, grad_kv
```

```python
import functools

import jax
import jax.numpy as jnp
from jax import lax
from jax.experimental import pallas as pl
from jax.experimental.pallas import tpu as pltpu
from jax.sharding import PartitionSpec as P

HD = 128
MESH = pl.DeviceIdType.MESH
LOG2E = 1.4426950408889634
NEG = -1e30


def kernel(
    n, sections, reach, heads_kv, group,
    q_ref, do_ref, kv_ref, docs_ref,
    dq_ref, out_ref,
    docs, qbuf, dobuf, kvbuf, bias, pbuf, dsbuf, sbuf, xbuf, tbuf, rbuf, dqbuf,
    docsem, lsem, qsend, qrecv, kvsend, kvrecv, fsend, frecv, xsend, xrecv, gsend, grecv, dqsend, dqrecv, dqloc,
):
    me = lax.axis_index("ctx")
    sec = lax.axis_index("section")
    rows = kv_ref.shape[1]
    layers = q_ref.shape[0] // rows
    width = group * layers * rows
    core = lax.rem(me, 2)
    other = 1 - core
    chip = me // 2
    chips = n // 2
    depth = reach // 2
    place = lax.rem(chip, depth)
    blocks = reach + 2
    heads = heads_kv // 2
    gw = group * HD
    window = (reach + 1) * rows
    piece = rows // sections
    scale = HD ** (-0.5)
    paired = sections % 2 == 0
    half = lax.rem(sec, 2)
    mate = sec + 1 - 2 * half

    def dev(ctx, section):
        return {"ctx": ctx, "section": section}

    def cols(head, width):
        return pl.ds(pl.multiple_of(head * width, HD), width)

    def local_copies(h):
        g = core * heads + h
        return [
            pltpu.make_async_copy(q_ref.at[:, cols(g, gw)], qbuf.at[h, core], lsem.at[h, 0]),
            pltpu.make_async_copy(do_ref.at[:, cols(g, gw)], dobuf.at[h, core], lsem.at[h, 1]),
            pltpu.make_async_copy(
                kv_ref.at[:, :, cols(g, HD)], kvbuf.at[h, :, reach + core], lsem.at[h, 2]
            ),
        ]

    def q_copies(h):
        g = other * heads + h
        partner = dev(2 * chip + other, sec)
        return [
            pltpu.make_async_remote_copy(
                src_ref=src.at[:, cols(g, gw)], dst_ref=dst.at[h, core],
                send_sem=qsend.at[h, k], recv_sem=qrecv.at[h, k],
                device_id=partner, device_id_type=MESH,
            )
            for k, (src, dst) in enumerate([(q_ref, qbuf), (do_ref, dobuf)])
        ]

    def kv_copy(h, d, w):
        to = lax.rem(core + w, 2)
        slot = core - 2 * d + reach
        return pltpu.make_async_remote_copy(
            src_ref=kv_ref.at[:, :, cols(to * heads + h, HD)], dst_ref=kvbuf.at[h, :, slot],
            send_sem=kvsend.at[h, d, w], recv_sem=kvrecv.at[h, slot],
            device_id=dev(2 * (chip + d) + to, sec), device_id_type=MESH,
        )

    def kv_half(h, w):
        to = lax.rem(core + w, 2)
        return pltpu.make_async_remote_copy(
            src_ref=kv_ref.at[half, :, cols(to * heads + h, HD)], dst_ref=kvbuf.at[h, half, core],
            send_sem=kvsend.at[h, depth, w], recv_sem=kvrecv.at[h, core],
            device_id=dev(2 * (chip + depth) + to, sec), device_id_type=MESH,
        )

    def kv_wait(h, slot):
        return pltpu.make_async_remote_copy(
            src_ref=kv_ref.at[:, :, pl.ds(0, HD)], dst_ref=kvbuf.at[h, :, slot],
            send_sem=kvsend.at[h, 0, 0], recv_sem=kvrecv.at[h, slot],
            device_id=dev(2 * chip + other, sec), device_id_type=MESH,
        )

    def half_wait(h, slot):
        return pltpu.make_async_remote_copy(
            src_ref=kv_ref.at[half, :, pl.ds(0, HD)], dst_ref=kvbuf.at[h, half, slot],
            send_sem=kvsend.at[h, 0, 0], recv_sem=kvrecv.at[h, slot],
            device_id=dev(2 * chip + other, sec), device_id_type=MESH,
        )

    def forward_copy(h, part):
        return pltpu.make_async_remote_copy(
            src_ref=kvbuf.at[h, part, pl.ds(0, 2)], dst_ref=kvbuf.at[h, part, pl.ds(0, 2)],
            send_sem=fsend.at[h], recv_sem=frecv.at[h],
            device_id=dev(me, mate), device_id_type=MESH,
        )

    def kv_sends(h, act):
        @pl.when(chip + depth < chips)
        def _():
            if paired:
                @pl.when(place >= 1)
                def _():
                    for w in range(2):
                        act(kv_half(h, w))

                @pl.when(place < 1)
                def _():
                    for w in range(2):
                        act(kv_copy(h, depth, w))
            else:
                for w in range(2):
                    act(kv_copy(h, depth, w))

        for d in range(depth - 1, 0, -1):
            @pl.when(chip + d < chips)
            def _():
                for w in range(2):
                    act(kv_copy(h, d, w))

    def start(copy):
        copy.start()

    def wait_send(copy):
        copy.wait_send()

    def forward(h):
        if paired:
            @pl.when((place >= 1) & (chip >= depth))
            def _():
                for slot in range(2):
                    half_wait(h, slot).wait_recv()
                forward_copy(h, half).start()

    def kv_arrivals(h):
        @pl.when(chip >= depth)
        def _():
            if paired:
                @pl.when(place >= 1)
                def _():
                    forward_copy(h, 1 - half).wait_recv()

                @pl.when(place < 1)
                def _():
                    for slot in range(2):
                        kv_wait(h, slot).wait_recv()
            else:
                for slot in range(2):
                    kv_wait(h, slot).wait_recv()

        for slot in range(2, reach):
            pl.when(2 * chip - reach + slot >= 0)(lambda: kv_wait(h, slot).wait_recv())
        for c in range(2):
            pl.when(core != c)(lambda: kv_wait(h, reach + c).wait_recv())

    def x_copy(h, pair, t, k):
        to = lax.rem(sec + t, sections)
        return pltpu.make_async_remote_copy(
            src_ref=sbuf.at[h, k, pl.ds(2 * pair, 2), pl.ds(pl.multiple_of(to * piece, piece), piece)],
            dst_ref=xbuf.at[h, t - 1, k, pl.ds(2 * pair, 2)],
            send_sem=xsend.at[h, pair, t - 1, k], recv_sem=xrecv.at[h, pair, t - 1, k],
            device_id=dev(me, to), device_id_type=MESH,
        )

    def g_copy(h, slot):
        d = (reach + 1 - slot) // 2
        return pltpu.make_async_remote_copy(
            src_ref=tbuf.at[h, slot], dst_ref=rbuf.at[d, core, h],
            send_sem=gsend.at[h, slot], recv_sem=grecv.at[d, core, h],
            device_id=dev(2 * (chip - d) + (slot - reach) % 2, sec), device_id_type=MESH,
        )

    def g_wait(h, d, c):
        return pltpu.make_async_remote_copy(
            src_ref=tbuf.at[h, 0], dst_ref=rbuf.at[d, c, h],
            send_sem=gsend.at[h, 0], recv_sem=grecv.at[d, c, h],
            device_id=dev(2 * chip + other, sec), device_id_type=MESH,
        )

    def when_pair(pair, run):
        if pair < depth:
            pl.when(chip >= depth - pair)(run)
        else:
            run()

    def when_sent(slot, run):
        if slot < reach:
            run()
        else:
            pl.when(core != slot - reach)(run)

    def scatter(h, k, pairs):
        def send(pair):
            for t in range(1, sections):
                x_copy(h, pair, t, k).start()

        for pair in pairs:
            when_pair(pair, functools.partial(send, pair))

    def deliver(h, pairs):
        own = pl.ds(pl.multiple_of(sec * piece, piece), piece)

        def run(pair):
            for t in range(1, sections):
                for k in range(2):
                    x_copy(h, pair, t, k).wait_recv()
            for slot in (2 * pair, 2 * pair + 1):
                total = sbuf[h, :, slot, own].astype(jnp.float32)
                for t in range(1, sections):
                    total = total + xbuf[h, t - 1, :, slot].astype(jnp.float32)
                tbuf[h, slot] = total.astype(jnp.bfloat16)
                when_sent(slot, lambda: g_copy(h, slot).start())

        for pair in pairs:
            when_pair(pair, functools.partial(run, pair))

    def dq_copy(h):
        return pltpu.make_async_remote_copy(
            src_ref=dqbuf.at[h, other], dst_ref=dq_ref.at[:, cols(core * heads + h, gw)],
            send_sem=dqsend.at[h], recv_sem=dqrecv.at[h],
            device_id=dev(2 * chip + other, sec), device_id_type=MESH,
        )

    def dq_wait(h):
        return pltpu.make_async_remote_copy(
            src_ref=dqbuf.at[h, other], dst_ref=dq_ref.at[:, cols(other * heads + h, gw)],
            send_sem=dqsend.at[h], recv_sem=dqrecv.at[h],
            device_id=dev(2 * chip + other, sec), device_id_type=MESH,
        )

    def dq_local(h):
        return pltpu.make_async_copy(
            dqbuf.at[h, core], dq_ref.at[:, cols(core * heads + h, gw)], dqloc.at[h]
        )

    barrier = pltpu.get_barrier_semaphore()

    def greet(ctx, section):
        pl.semaphore_signal(barrier, inc=1, device_id=dev(ctx, section), device_id_type=MESH)

    for t in range(1, sections):
        greet(me, lax.rem(sec + t, sections))
    for step in range(-depth, depth + 1):
        @pl.when((chip + step >= 0) & (chip + step < chips))
        def _():
            for w in range(2):
                if step == 0 and w == 0:
                    continue
                greet(2 * (chip + step) + lax.rem(core + w, 2), sec)

    docs_copy = pltpu.make_async_copy(docs_ref, docs, docsem)
    docs_copy.start()
    for h in range(heads):
        for copy in local_copies(h):
            copy.start()

    near = jnp.minimum(chip, depth) + jnp.minimum(chips - 1 - chip, depth)
    pl.semaphore_wait(barrier, 2 * near + 1 + sections - 1)

    def all_sends(h):
        kv_sends(h, start)
        kv_copy(h, 0, 1).start()
        for copy in q_copies(h):
            copy.start()

    all_sends(0)

    for d in range(1, depth + 1):
        @pl.when(chip - d < 0)
        def _():
            for slot in (reach - 2 * d, reach - 2 * d + 1):
                for h in range(heads):
                    kvbuf[h, :, slot] = jnp.zeros((2, rows, HD), jnp.bfloat16)

        @pl.when(chip + d >= chips)
        def _():
            rbuf[d] = jnp.zeros(rbuf.shape[1:], jnp.bfloat16)

    docs_copy.wait()
    row_at = lax.broadcasted_iota(jnp.int32, (rows, rows), 0)
    col_at = lax.broadcasted_iota(jnp.int32, (rows, rows), 1)
    for slot in range(blocks):
        at = 2 * chip - reach + slot
        kdoc = docs[pl.ds(jnp.maximum(at, 0), 1), :].astype(jnp.float32)
        kdoc = jnp.transpose(jnp.broadcast_to(kdoc, (rows, rows)))
        for sub in range(2):
            if not 0 <= slot - sub <= reach:
                continue
            qdoc = docs[pl.ds(2 * chip + sub, 1), :].astype(jnp.float32)
            kplace = at * rows + row_at
            qplace = (2 * chip + sub) * rows + col_at
            seen = (kplace <= qplace) & (kplace >= 0) & (kdoc == qdoc)
            bias[sub, (slot - sub) * rows : (slot - sub + 1) * rows] = jnp.where(seen, 0.0, NEG)

    def score_part(h, sub):
        k = kvbuf[h, 0, pl.ds(sub, reach + 1)].reshape(window, HD)
        v = kvbuf[h, 1, pl.ds(sub, reach + 1)].reshape(window, HD)
        keys_at = pl.ds(pl.multiple_of(sub * rows, rows), window)
        nt = (((1,), (1,)), ((), ()))
        for i in range(group):
            at = slice(i * HD, (i + 1) * HD)
            s = lax.dot_general(k, qbuf[h, sub, :, at], nt, preferred_element_type=jnp.float32)
            dp = lax.dot_general(v, dobuf[h, sub, :, at], nt, preferred_element_type=jnp.float32)
            s = s * (scale * LOG2E) + jnp.concatenate([bias[sub]] * layers, axis=1)
            e = jnp.exp2(s - jnp.max(s, axis=0, keepdims=True))
            inverse = 1.0 / jnp.sum(e, axis=0, keepdims=True)
            delta = jnp.sum(e * dp, axis=0, keepdims=True) * inverse
            p = (e * inverse).astype(jnp.bfloat16)
            to = slice(i * layers * rows, (i + 1) * layers * rows)
            pbuf[sub, keys_at, to] = p
            dsbuf[h, sub, keys_at, to] = (p.astype(jnp.float32) * (dp - delta)).astype(jnp.bfloat16)

    def stacked(h, k, sub):
        buf = (qbuf, dobuf)[k]
        return jnp.concatenate([buf[h, sub, :, i * HD : (i + 1) * HD] for i in range(group)], axis=0)

    def key_part(h, k, low, high):
        stacks = [stacked(h, k, sub) for sub in range(2)]
        at = slice(low * rows, high * rows)
        total = 0.0
        for sub in range(2):
            weights = dsbuf[h, sub, at] if k == 0 else pbuf[sub, at]
            total = total + jnp.dot(weights, stacks[sub], preferred_element_type=jnp.float32)
        total = total * scale if k == 0 else total
        sbuf[h, k, low:high] = total.astype(jnp.bfloat16).reshape(high - low, rows, HD)

    def edge_part(h, k, slot, sub):
        at = slice(slot * rows, (slot + 1) * rows)
        weights = dsbuf[h, sub, at] if k == 0 else pbuf[sub, at]
        total = jnp.dot(weights, stacked(h, k, sub), preferred_element_type=jnp.float32)
        sbuf[h, k, slot] = (total * scale if k == 0 else total).astype(jnp.bfloat16)

    def query_part(h, sub):
        kt = jnp.transpose(kvbuf[h, 0, pl.ds(sub, reach + 1)].reshape(window, HD))
        keys_at = pl.ds(pl.multiple_of(sub * rows, rows), window)
        dqt = jnp.dot(kt, dsbuf[h, sub, keys_at], preferred_element_type=jnp.float32) * scale
        for i in range(group):
            dqbuf[h, sub, :, i * HD : (i + 1) * HD] = jnp.transpose(
                dqt[:, i * layers * rows : (i + 1) * layers * rows]
            ).astype(jnp.bfloat16)

    def sent_kv(h):
        kv_sends(h, wait_send)

    forward(0)
    sent_kv(0)
    for h in range(1, heads):
        all_sends(h)

    def head_step(h, unused):
        local_copies(h)[2].wait()
        kv_arrivals(h)
        for copy in local_copies(h)[:2]:
            copy.wait()
        score_part(h, core)
        pl.when(h + 1 < heads)(lambda: forward(h + 1))
        for copy in q_copies(h):
            copy.wait_recv()
        score_part(h, other)
        for k in (1, 0):
            edge_part(h, k, 0, 0)
            key_part(h, k, 1, reach)
            scatter(h, k, range(depth))
        for k in (1, 0):
            key_part(h, k, reach, reach + 1)
            edge_part(h, k, reach + 1, 1)
            scatter(h, k, range(depth, depth + 1))
        pl.when(h > 0)(lambda: deliver(h - 1, range(depth)))
        return unused

    lax.fori_loop(0, heads, head_step, 0)

    def query_step(h, unused):
        query_part(h, other)
        dq_copy(h).start()
        query_part(h, core)
        dq_local(h).start()
        return unused

    lax.fori_loop(0, heads, query_step, 0)
    deliver(heads - 1, range(depth))

    def own_step(h, unused):
        deliver(h, range(depth, depth + 1))
        rbuf[0, core, h] = tbuf[h, reach + core]
        return unused

    lax.fori_loop(0, heads, own_step, 0)

    for h in range(heads):
        for c in range(2):
            for d in range(depth, -1, -1):
                pl.when(core != c if d == 0 else chip + d < chips)(lambda: g_wait(h, d, c).wait_recv())
            total = rbuf[0, c, h].astype(jnp.float32)
            for d in range(1, depth + 1):
                total = total + rbuf[d, c, h].astype(jnp.float32)
            g = c * heads + h
            out_ref[:, :, g * HD : (g + 1) * HD] = total.astype(jnp.bfloat16)

    def finish(h, unused):
        dq_wait(h).wait_recv()
        dq_copy(h).wait_send()
        dq_local(h).wait()
        for copy in q_copies(h):
            copy.wait_send()
        kv_copy(h, 0, 1).wait_send()
        pl.when(h > 0)(lambda: sent_kv(h))
        if paired:
            @pl.when((place >= 1) & (chip >= depth))
            def _():
                forward_copy(h, half).wait_send()

        def sent(pair):
            for t in range(1, sections):
                for k in range(2):
                    x_copy(h, pair, t, k).wait_send()
            for slot in (2 * pair, 2 * pair + 1):
                when_sent(slot, lambda: g_copy(h, slot).wait_send())

        for pair in range(depth + 1):
            when_pair(pair, functools.partial(sent, pair))
        return unused

    lax.fori_loop(0, heads, finish, 0)


def body(queries, grad_out, keys_values, doc_ids):
    layers, rows, width = queries.shape
    kv_width = keys_values.shape[2]
    heads_kv = kv_width // HD
    group = width // kv_width
    n = lax.axis_size("ctx")
    sections = lax.axis_size("section")
    reach = n // 4
    heads = heads_kv // 2
    blocks = reach + 2
    window = (reach + 1) * rows
    piece = rows // sections
    depth = reach // 2
    bf, f32 = jnp.bfloat16, jnp.float32
    dma = pltpu.SemaphoreType.DMA
    hbm = pl.BlockSpec(memory_space=pl.ANY)
    vmem = pl.BlockSpec(memory_space=pltpu.VMEM)
    grad_queries, grad_kv = pl.pallas_call(
        functools.partial(kernel, n, sections, reach, heads_kv, group),
        out_shape=(
            jax.ShapeDtypeStruct((layers * rows, width), bf),
            jax.ShapeDtypeStruct((2, piece, kv_width), bf),
        ),
        in_specs=[hbm, hbm, hbm, hbm],
        out_specs=(hbm, vmem),
        scratch_shapes=[
            pltpu.VMEM((n, rows), jnp.int32),
            pltpu.VMEM((heads, 2, layers * rows, group * HD), bf),
            pltpu.VMEM((heads, 2, layers * rows, group * HD), bf),
            pltpu.VMEM((heads, 2, blocks, rows, HD), bf),
            pltpu.VMEM((2, window, rows), f32),
            pltpu.VMEM((2, blocks * rows, group * layers * rows), bf),
            pltpu.VMEM((heads, 2, blocks * rows, group * layers * rows), bf),
            pltpu.VMEM((heads, 2, blocks, rows, HD), bf),
            pltpu.VMEM((heads, max(sections - 1, 1), 2, blocks, piece, HD), bf),
            pltpu.VMEM((heads, blocks, 2, piece, HD), bf),
            pltpu.VMEM((depth + 1, 2, heads, 2, piece, HD), bf),
            pltpu.VMEM((heads, 2, layers * rows, group * HD), bf),
            dma,
            dma((heads, 3)),
            dma((heads, 2)),
            dma((heads, 2)),
            dma((heads, depth + 1, 2)),
            dma((heads, blocks)),
            dma((heads,)),
            dma((heads,)),
            dma((heads, depth + 1, max(sections - 1, 1), 2)),
            dma((heads, depth + 1, max(sections - 1, 1), 2)),
            dma((heads, blocks)),
            dma((depth + 1, 2, heads)),
            dma((heads,)),
            dma((heads,)),
            dma((heads,)),
        ],
        compiler_params=pltpu.CompilerParams(
            collective_id=0, has_side_effects=True, vmem_limit_bytes=40 * 1024 * 1024
        ),
        name="cross_backward",
    )(
        *[
            pltpu.with_memory_space_constraint(x, pltpu.HBM)
            for x in (
                queries.reshape(layers * rows, width), grad_out.reshape(layers * rows, width),
                keys_values, doc_ids.reshape(n, rows),
            )
        ]
    )
    return grad_queries.reshape(queries.shape), grad_kv


def solution(mesh):
    return jax.shard_map(
        body,
        mesh=mesh,
        in_specs=(P("section", "ctx", None), P("section", "ctx", None), P(None, "ctx", None), P()),
        out_specs=(P("section", "ctx", None), P(None, ("ctx", "section"), None)),
        check_vma=False,
    )
```

```python
import functools

import jax
import jax.numpy as jnp
from jax import lax
from jax.experimental import pallas as pl
from jax.experimental.pallas import tpu as pltpu
from jax.sharding import PartitionSpec as P

HD = 128
MESH = pl.DeviceIdType.MESH
LOG2E = 1.4426950408889634
NEG = -1e30


def kernel(
    n, sections, reach, heads_kv, group,
    q_ref, do_ref, kv_ref, docs_ref,
    dq_ref, out_ref,
    docs, qbuf, dobuf, kvbuf, bias, ebuf, dpbuf, stat, pbuf, dsbuf, sbuf, xbuf, tbuf, rbuf, dqbuf,
    docsem, lsem, qsend, qrecv, kvsend, kvrecv, fsend, frecv, xsend, xrecv, gsend, grecv, dqsend, dqrecv, dqloc,
):
    me = lax.axis_index("ctx")
    sec = lax.axis_index("section")
    rows = kv_ref.shape[1]
    layers = q_ref.shape[0] // rows
    width = group * layers * rows
    core = lax.rem(me, 2)
    other = 1 - core
    chip = me // 2
    chips = n // 2
    depth = reach // 2
    place = lax.rem(chip, depth)
    blocks = reach + 2
    heads = heads_kv // 2
    gw = group * HD
    window = (reach + 1) * rows
    piece = rows // sections
    scale = HD ** (-0.5)
    paired = sections % 2 == 0
    half = lax.rem(sec, 2)
    mate = sec + 1 - 2 * half

    def dev(ctx, section):
        return {"ctx": ctx, "section": section}

    def cols(head, width):
        return pl.ds(pl.multiple_of(head * width, HD), width)

    def local_copies(h):
        g = core * heads + h
        return [
            pltpu.make_async_copy(q_ref.at[:, cols(g, gw)], qbuf.at[h, core], lsem.at[h, 0]),
            pltpu.make_async_copy(do_ref.at[:, cols(g, gw)], dobuf.at[h, core], lsem.at[h, 1]),
            pltpu.make_async_copy(
                kv_ref.at[:, :, cols(g, HD)], kvbuf.at[h, :, reach + core], lsem.at[h, 2]
            ),
        ]

    def q_copies(h):
        g = other * heads + h
        partner = dev(2 * chip + other, sec)
        return [
            pltpu.make_async_remote_copy(
                src_ref=src.at[:, cols(g, gw)], dst_ref=dst.at[h, core],
                send_sem=qsend.at[h, k], recv_sem=qrecv.at[h, k],
                device_id=partner, device_id_type=MESH,
            )
            for k, (src, dst) in enumerate([(q_ref, qbuf), (do_ref, dobuf)])
        ]

    def kv_copy(h, d, w):
        to = lax.rem(core + w, 2)
        slot = core - 2 * d + reach
        return pltpu.make_async_remote_copy(
            src_ref=kv_ref.at[:, :, cols(to * heads + h, HD)], dst_ref=kvbuf.at[h, :, slot],
            send_sem=kvsend.at[h, d, w], recv_sem=kvrecv.at[h, slot],
            device_id=dev(2 * (chip + d) + to, sec), device_id_type=MESH,
        )

    def kv_half(h, w):
        to = lax.rem(core + w, 2)
        return pltpu.make_async_remote_copy(
            src_ref=kv_ref.at[half, :, cols(to * heads + h, HD)], dst_ref=kvbuf.at[h, half, core],
            send_sem=kvsend.at[h, depth, w], recv_sem=kvrecv.at[h, core],
            device_id=dev(2 * (chip + depth) + to, sec), device_id_type=MESH,
        )

    def kv_wait(h, slot):
        return pltpu.make_async_remote_copy(
            src_ref=kv_ref.at[:, :, pl.ds(0, HD)], dst_ref=kvbuf.at[h, :, slot],
            send_sem=kvsend.at[h, 0, 0], recv_sem=kvrecv.at[h, slot],
            device_id=dev(2 * chip + other, sec), device_id_type=MESH,
        )

    def half_wait(h, slot):
        return pltpu.make_async_remote_copy(
            src_ref=kv_ref.at[half, :, pl.ds(0, HD)], dst_ref=kvbuf.at[h, half, slot],
            send_sem=kvsend.at[h, 0, 0], recv_sem=kvrecv.at[h, slot],
            device_id=dev(2 * chip + other, sec), device_id_type=MESH,
        )

    def forward_copy(h, part):
        return pltpu.make_async_remote_copy(
            src_ref=kvbuf.at[h, part, pl.ds(0, 2)], dst_ref=kvbuf.at[h, part, pl.ds(0, 2)],
            send_sem=fsend.at[h], recv_sem=frecv.at[h],
            device_id=dev(me, mate), device_id_type=MESH,
        )

    def far_sends(h, act):
        @pl.when(chip + depth < chips)
        def _():
            if paired:
                @pl.when(place >= 1)
                def _():
                    for w in range(2):
                        act(kv_half(h, w))

                @pl.when(place < 1)
                def _():
                    for w in range(2):
                        act(kv_copy(h, depth, w))
            else:
                for w in range(2):
                    act(kv_copy(h, depth, w))

    def near_sends(h, act):
        for d in range(depth - 1, 0, -1):
            @pl.when(chip + d < chips)
            def _():
                for w in range(2):
                    act(kv_copy(h, d, w))

    def start(copy):
        copy.start()

    def wait_send(copy):
        copy.wait_send()

    def forward(h):
        if paired:
            @pl.when((place >= 1) & (chip >= depth))
            def _():
                for slot in range(2):
                    half_wait(h, slot).wait_recv()
                forward_copy(h, half).start()

    def kv_arrivals(h):
        @pl.when(chip >= depth)
        def _():
            if paired:
                @pl.when(place >= 1)
                def _():
                    forward_copy(h, 1 - half).wait_recv()

                @pl.when(place < 1)
                def _():
                    for slot in range(2):
                        kv_wait(h, slot).wait_recv()
            else:
                for slot in range(2):
                    kv_wait(h, slot).wait_recv()

        for slot in range(2, reach):
            pl.when(2 * chip - reach + slot >= 0)(lambda: kv_wait(h, slot).wait_recv())
    def x_copy(h, pair, t, k):
        to = lax.rem(sec + t, sections)
        return pltpu.make_async_remote_copy(
            src_ref=sbuf.at[h, k, pl.ds(2 * pair, 2), pl.ds(pl.multiple_of(to * piece, piece), piece)],
            dst_ref=xbuf.at[h, t - 1, k, pl.ds(2 * pair, 2)],
            send_sem=xsend.at[h, pair, t - 1, k], recv_sem=xrecv.at[h, pair, t - 1, k],
            device_id=dev(me, to), device_id_type=MESH,
        )

    def g_copy(h, k, slot):
        d = (reach + 1 - slot) // 2
        return pltpu.make_async_remote_copy(
            src_ref=tbuf.at[h, slot, k], dst_ref=rbuf.at[d, core, h, k],
            send_sem=gsend.at[h, slot, k], recv_sem=grecv.at[d, core, h, k],
            device_id=dev(2 * (chip - d) + (slot - reach) % 2, sec), device_id_type=MESH,
        )

    def g_wait(h, k, d, c):
        return pltpu.make_async_remote_copy(
            src_ref=tbuf.at[h, 0, k], dst_ref=rbuf.at[d, c, h, k],
            send_sem=gsend.at[h, 0, k], recv_sem=grecv.at[d, c, h, k],
            device_id=dev(2 * chip + other, sec), device_id_type=MESH,
        )

    def when_pair(pair, run):
        if pair < depth:
            pl.when(chip >= depth - pair)(run)
        else:
            run()

    def when_sent(slot, run):
        if slot < reach:
            run()
        else:
            pl.when(core != slot - reach)(run)

    def scatter(h, k, pairs):
        def send(pair):
            for t in range(1, sections):
                x_copy(h, pair, t, k).start()

        for pair in pairs:
            when_pair(pair, functools.partial(send, pair))

    def deliver(h, k, pairs):
        own = pl.ds(pl.multiple_of(sec * piece, piece), piece)

        def run(pair):
            for t in range(1, sections):
                x_copy(h, pair, t, k).wait_recv()
            for slot in (2 * pair, 2 * pair + 1):
                total = sbuf[h, k, slot, own].astype(jnp.float32)
                for t in range(1, sections):
                    total = total + xbuf[h, t - 1, k, slot].astype(jnp.float32)
                tbuf[h, slot, k] = total.astype(jnp.bfloat16)
                when_sent(slot, lambda: g_copy(h, k, slot).start())

        for pair in pairs:
            when_pair(pair, functools.partial(run, pair))

    def dq_copy(h):
        return pltpu.make_async_remote_copy(
            src_ref=dqbuf.at[h, other], dst_ref=dq_ref.at[:, cols(core * heads + h, gw)],
            send_sem=dqsend.at[h], recv_sem=dqrecv.at[h],
            device_id=dev(2 * chip + other, sec), device_id_type=MESH,
        )

    def dq_wait(h):
        return pltpu.make_async_remote_copy(
            src_ref=dqbuf.at[h, other], dst_ref=dq_ref.at[:, cols(other * heads + h, gw)],
            send_sem=dqsend.at[h], recv_sem=dqrecv.at[h],
            device_id=dev(2 * chip + other, sec), device_id_type=MESH,
        )

    def dq_local(h):
        return pltpu.make_async_copy(
            dqbuf.at[h, core], dq_ref.at[:, cols(core * heads + h, gw)], dqloc.at[h]
        )

    barrier = pltpu.get_barrier_semaphore()

    def greet(ctx, section):
        pl.semaphore_signal(barrier, inc=1, device_id=dev(ctx, section), device_id_type=MESH)

    for t in range(1, sections):
        greet(me, lax.rem(sec + t, sections))
    for step in range(-depth, depth + 1):
        @pl.when((chip + step >= 0) & (chip + step < chips))
        def _():
            for w in range(2):
                if step == 0 and w == 0:
                    continue
                greet(2 * (chip + step) + lax.rem(core + w, 2), sec)

    docs_copy = pltpu.make_async_copy(docs_ref, docs, docsem)
    docs_copy.start()
    for h in range(heads):
        for copy in local_copies(h):
            copy.start()

    near = jnp.minimum(chip, depth) + jnp.minimum(chips - 1 - chip, depth)
    pl.semaphore_wait(barrier, 2 * near + 1 + sections - 1)

    far_sends(0, start)
    near_sends(0, start)
    for h in range(heads):
        kv_copy(h, 0, 1).start()
        for copy in q_copies(h):
            copy.start()

    for d in range(1, depth + 1):
        @pl.when(chip - d < 0)
        def _():
            for slot in (reach - 2 * d, reach - 2 * d + 1):
                for h in range(heads):
                    kvbuf[h, :, slot] = jnp.zeros((2, rows, HD), jnp.bfloat16)

        @pl.when(chip + d >= chips)
        def _():
            rbuf[d] = jnp.zeros(rbuf.shape[1:], jnp.bfloat16)

    for h in range(heads):
        dsbuf[h, 0:rows, width : 2 * width] = jnp.zeros((rows, width), jnp.bfloat16)
        dsbuf[h, (reach + 1) * rows : blocks * rows, 0:width] = jnp.zeros((rows, width), jnp.bfloat16)
    docs_copy.wait()
    row_at = lax.broadcasted_iota(jnp.int32, (rows, rows), 0)
    col_at = lax.broadcasted_iota(jnp.int32, (rows, rows), 1)
    for slot in range(blocks):
        at = 2 * chip - reach + slot
        kdoc = docs[pl.ds(jnp.maximum(at, 0), 1), :].astype(jnp.float32)
        kdoc = jnp.transpose(jnp.broadcast_to(kdoc, (rows, rows)))
        for sub in range(2):
            if not 0 <= slot - sub <= reach:
                continue
            qdoc = docs[pl.ds(2 * chip + sub, 1), :].astype(jnp.float32)
            kplace = at * rows + row_at
            qplace = (2 * chip + sub) * rows + col_at
            seen = (kplace <= qplace) & (kplace >= 0) & (kdoc == qdoc)
            bias[sub, (slot - sub) * rows : (slot - sub + 1) * rows] = jnp.where(seen, 0.0, NEG)

    def stacked(h, k, sub):
        buf = (qbuf, dobuf)[k]
        return jnp.concatenate([buf[h, sub, :, i * HD : (i + 1) * HD] for i in range(group)], axis=0)

    def part_rows(sub, part):
        first = (reach - sub) * rows
        return slice(first, window) if part == 0 else slice(0, first)

    def score_part(h, sub, part):
        at = part_rows(sub, part)
        slots = slice(at.start // rows + sub, at.stop // rows + sub)
        k = kvbuf[h, 0, slots].reshape(at.stop - at.start, HD)
        v = kvbuf[h, 1, slots].reshape(at.stop - at.start, HD)
        nt = (((1,), (1,)), ((), ()))
        s = lax.dot_general(k, stacked(h, 0, sub), nt, preferred_element_type=jnp.float32)
        dp = lax.dot_general(v, stacked(h, 1, sub), nt, preferred_element_type=jnp.float32)
        s = s * (scale * LOG2E) + jnp.concatenate([bias[sub, at]] * (layers * group), axis=1)
        top = jnp.max(s, axis=0, keepdims=True)
        e = jnp.exp2(s - top)
        ebuf[h, sub, at] = e
        dpbuf[h, sub, at] = dp
        stat[h, sub, part, 0:1] = top
        stat[h, sub, part, 1:2] = jnp.sum(e, axis=0, keepdims=True)
        stat[h, sub, part, 2:3] = jnp.sum(e * dp, axis=0, keepdims=True)

    def prob_part(h, sub):
        tops = [stat[h, sub, part, 0:1] for part in range(2)]
        top = jnp.maximum(*tops)
        factors = [jnp.exp2(t - top) for t in tops]
        total = factors[0] * stat[h, sub, 0, 1:2] + factors[1] * stat[h, sub, 1, 1:2]
        factors = [f / total for f in factors]
        delta = factors[0] * stat[h, sub, 0, 2:3] + factors[1] * stat[h, sub, 1, 2:3]
        for part in range(2):
            at = part_rows(sub, part)
            keys_at = slice(at.start + sub * rows, at.stop + sub * rows)
            for i in range(group):
                span = slice(i * layers * rows, (i + 1) * layers * rows)
                p = ebuf[h, sub, at, span] * factors[part][:, span]
                ds = p * (dpbuf[h, sub, at, span] - delta[:, span])
                to = slice(sub * width + span.start, sub * width + span.stop)
                pbuf[keys_at, to] = p.astype(jnp.bfloat16)
                dsbuf[h, keys_at, to] = ds.astype(jnp.bfloat16)

    def key_part(h, k):
        stack = jnp.concatenate([stacked(h, k, sub) for sub in range(2)], axis=0)
        at = slice(rows, (reach + 1) * rows)
        total = jnp.dot(dsbuf[h, at] if k == 0 else pbuf[at], stack, preferred_element_type=jnp.float32)
        total = total * scale if k == 0 else total
        sbuf[h, k, 1 : reach + 1] = total.astype(jnp.bfloat16).reshape(reach, rows, HD)

    def edge_part(h, k, slot, sub):
        at = slice(slot * rows, (slot + 1) * rows)
        to = slice(sub * width, (sub + 1) * width)
        weights = dsbuf[h, at, to] if k == 0 else pbuf[at, to]
        total = jnp.dot(weights, stacked(h, k, sub), preferred_element_type=jnp.float32)
        sbuf[h, k, slot] = (total * scale if k == 0 else total).astype(jnp.bfloat16)

    def query_part(h, sub):
        kt = jnp.transpose(kvbuf[h, 0].reshape(blocks * rows, HD))
        to = pl.ds(pl.multiple_of(sub * width, rows), width)
        dqt = jnp.dot(kt, dsbuf[h, :, to], preferred_element_type=jnp.float32) * scale
        for i in range(group):
            dqbuf[h, sub, :, i * HD : (i + 1) * HD] = jnp.transpose(
                dqt[:, i * layers * rows : (i + 1) * layers * rows]
            ).astype(jnp.bfloat16)

    def own_scores(h, unused):
        for copy in local_copies(h):
            copy.wait()
        for copy in q_copies(h):
            copy.wait_recv()
        for c in range(2):
            pl.when(core != c)(lambda: kv_wait(h, reach + c).wait_recv())
        for sub in range(2):
            score_part(h, sub, 0)
        return unused

    lax.fori_loop(0, heads, own_scores, 0)

    forward(0)
    for h in range(1, heads):
        far_sends(h - 1, wait_send)
        far_sends(h, start)
        near_sends(h - 1, wait_send)
        near_sends(h, start)

    def head_step(h, unused):
        kv_arrivals(h)
        score_part(h, 0, 1)
        pl.when(h + 1 < heads)(lambda: forward(h + 1))
        prob_part(h, 0)
        score_part(h, 1, 1)
        prob_part(h, 1)
        for k in (1, 0):
            pl.when(h > 0)(lambda: deliver(h - 1, k, far))
            key_part(h, k)
            edge_part(h, k, 0, 0)
            scatter(h, k, far)
        for k in (1, 0):
            edge_part(h, k, reach + 1, 1)
        pl.when(h + 1 < heads)(lambda: scatter(h, 1, near))
        return unused

    far, near = range(depth), range(depth, depth + 1)
    lax.fori_loop(0, heads, head_step, 0)
    last = heads - 1
    for h in range(heads):
        for k in (1, 0):
            if h == last or k == 0:
                scatter(h, k, near)
    def queries(h):
        query_part(h, other)
        dq_copy(h).start()
        query_part(h, core)
        dq_local(h).start()

    for h in range(last):
        queries(h)
    deliver(last, 1, far)
    queries(last)
    deliver(last, 0, far)

    def own_step(h, unused):
        for k in (1, 0):
            deliver(h, k, near)
            rbuf[0, core, h, k] = tbuf[h, reach + core, k]
        return unused

    lax.fori_loop(0, heads, own_step, 0)

    for h in range(heads):
        for k in (1, 0):
            for c in range(2):
                for d in range(depth, -1, -1):
                    pl.when(core != c if d == 0 else chip + d < chips)(lambda: g_wait(h, k, d, c).wait_recv())
                total = rbuf[0, c, h, k].astype(jnp.float32)
                for d in range(1, depth + 1):
                    total = total + rbuf[d, c, h, k].astype(jnp.float32)
                g = c * heads + h
                out_ref[k, :, g * HD : (g + 1) * HD] = total.astype(jnp.bfloat16)

    def finish(h, unused):
        dq_wait(h).wait_recv()
        dq_copy(h).wait_send()
        dq_local(h).wait()
        for copy in q_copies(h):
            copy.wait_send()
        kv_copy(h, 0, 1).wait_send()
        pl.when(h == heads - 1)(lambda: far_sends(h, wait_send))
        pl.when(h == heads - 1)(lambda: near_sends(h, wait_send))
        if paired:
            @pl.when((place >= 1) & (chip >= depth))
            def _():
                forward_copy(h, half).wait_send()

        def sent(pair):
            for t in range(1, sections):
                for k in range(2):
                    x_copy(h, pair, t, k).wait_send()
            for slot in (2 * pair, 2 * pair + 1):
                for k in range(2):
                    when_sent(slot, lambda: g_copy(h, k, slot).wait_send())

        for pair in range(depth + 1):
            when_pair(pair, functools.partial(sent, pair))
        return unused

    lax.fori_loop(0, heads, finish, 0)


def body(queries, grad_out, keys_values, doc_ids):
    layers, rows, width = queries.shape
    kv_width = keys_values.shape[2]
    heads_kv = kv_width // HD
    group = width // kv_width
    n = lax.axis_size("ctx")
    sections = lax.axis_size("section")
    reach = n // 4
    heads = heads_kv // 2
    blocks = reach + 2
    window = (reach + 1) * rows
    piece = rows // sections
    depth = reach // 2
    bf, f32 = jnp.bfloat16, jnp.float32
    dma = pltpu.SemaphoreType.DMA
    hbm = pl.BlockSpec(memory_space=pl.ANY)
    vmem = pl.BlockSpec(memory_space=pltpu.VMEM)
    grad_queries, grad_kv = pl.pallas_call(
        functools.partial(kernel, n, sections, reach, heads_kv, group),
        out_shape=(
            jax.ShapeDtypeStruct((layers * rows, width), bf),
            jax.ShapeDtypeStruct((2, piece, kv_width), bf),
        ),
        in_specs=[hbm, hbm, hbm, hbm],
        out_specs=(hbm, vmem),
        scratch_shapes=[
            pltpu.VMEM((n, rows), jnp.int32),
            pltpu.VMEM((heads, 2, layers * rows, group * HD), bf),
            pltpu.VMEM((heads, 2, layers * rows, group * HD), bf),
            pltpu.VMEM((heads, 2, blocks, rows, HD), bf),
            pltpu.VMEM((2, window, rows), f32),
            pltpu.VMEM((heads, 2, window, group * layers * rows), f32),
            pltpu.VMEM((heads, 2, window, group * layers * rows), f32),
            pltpu.VMEM((heads, 2, 2, 8, group * layers * rows), f32),
            pltpu.VMEM((blocks * rows, 2 * group * layers * rows), bf),
            pltpu.VMEM((heads, blocks * rows, 2 * group * layers * rows), bf),
            pltpu.VMEM((heads, 2, blocks, rows, HD), bf),
            pltpu.VMEM((heads, max(sections - 1, 1), 2, blocks, piece, HD), bf),
            pltpu.VMEM((heads, blocks, 2, piece, HD), bf),
            pltpu.VMEM((depth + 1, 2, heads, 2, piece, HD), bf),
            pltpu.VMEM((heads, 2, layers * rows, group * HD), bf),
            dma,
            dma((heads, 3)),
            dma((heads, 2)),
            dma((heads, 2)),
            dma((heads, depth + 1, 2)),
            dma((heads, blocks)),
            dma((heads,)),
            dma((heads,)),
            dma((heads, depth + 1, max(sections - 1, 1), 2)),
            dma((heads, depth + 1, max(sections - 1, 1), 2)),
            dma((heads, blocks, 2)),
            dma((depth + 1, 2, heads, 2)),
            dma((heads,)),
            dma((heads,)),
            dma((heads,)),
        ],
        compiler_params=pltpu.CompilerParams(
            collective_id=0, has_side_effects=True, vmem_limit_bytes=(24 + 4 * reach) * 1024 * 1024
        ),
        name="cross_backward",
    )(
        *[
            pltpu.with_memory_space_constraint(x, pltpu.HBM)
            for x in (
                queries.reshape(layers * rows, width), grad_out.reshape(layers * rows, width),
                keys_values, doc_ids.reshape(n, rows),
            )
        ]
    )
    return grad_queries.reshape(queries.shape), grad_kv


def solution(mesh):
    return jax.shard_map(
        body,
        mesh=mesh,
        in_specs=(P("section", "ctx", None), P("section", "ctx", None), P(None, "ctx", None), P()),
        out_specs=(P("section", "ctx", None), P(None, ("ctx", "section"), None)),
        check_vma=False,
    )
```

```python
import functools

import jax
import jax.numpy as jnp
from jax import lax
from jax.experimental import pallas as pl
from jax.experimental.pallas import tpu as pltpu
from jax.sharding import PartitionSpec as P

HD = 128
MESH = pl.DeviceIdType.MESH
LOG2E = 1.4426950408889634
NEG = -1e30


def kernel(
    n, sections, reach, heads_kv, group,
    q_ref, do_ref, kv_ref, docs_ref,
    dq_ref, out_ref,
    docs, qbuf, dobuf, kvbuf, bias, ebuf, dpbuf, stat, pbuf, dsbuf, sbuf, ubuf, xbuf, tbuf, rbuf, dqbuf,
    docsem, lsem, qsend, qrecv, kvsend, kvrecv, fsend, frecv, usend, urecv, xsend, xrecv, gsend, grecv, dqsend, dqrecv, dqloc,
):
    me = lax.axis_index("ctx")
    sec = lax.axis_index("section")
    rows = kv_ref.shape[1]
    layers = q_ref.shape[0] // rows
    width = group * layers * rows
    core = lax.rem(me, 2)
    other = 1 - core
    chip = me // 2
    chips = n // 2
    depth = reach // 2
    place = lax.rem(chip, depth)
    blocks = reach + 2
    heads = heads_kv // 2
    gw = group * HD
    window = (reach + 1) * rows
    piece = rows // sections
    scale = HD ** (-0.5)
    paired = sections % 2 == 0
    half = lax.rem(sec, 2)
    mate = sec + 1 - 2 * half

    def dev(ctx, section):
        return {"ctx": ctx, "section": section}

    def cols(head, width):
        return pl.ds(pl.multiple_of(head * width, HD), width)

    def local_copies(h):
        g = core * heads + h
        return [
            pltpu.make_async_copy(q_ref.at[:, cols(g, gw)], qbuf.at[h, core], lsem.at[h, 0]),
            pltpu.make_async_copy(do_ref.at[:, cols(g, gw)], dobuf.at[h, core], lsem.at[h, 1]),
            pltpu.make_async_copy(
                kv_ref.at[:, :, cols(g, HD)], kvbuf.at[h, :, reach + core], lsem.at[h, 2]
            ),
        ]

    def q_copies(h):
        g = other * heads + h
        partner = dev(2 * chip + other, sec)
        return [
            pltpu.make_async_remote_copy(
                src_ref=src.at[:, cols(g, gw)], dst_ref=dst.at[h, core],
                send_sem=qsend.at[h, k], recv_sem=qrecv.at[h, k],
                device_id=partner, device_id_type=MESH,
            )
            for k, (src, dst) in enumerate([(q_ref, qbuf), (do_ref, dobuf)])
        ]

    def kv_copy(h, d, w):
        to = lax.rem(core + w, 2)
        slot = core - 2 * d + reach
        return pltpu.make_async_remote_copy(
            src_ref=kv_ref.at[:, :, cols(to * heads + h, HD)], dst_ref=kvbuf.at[h, :, slot],
            send_sem=kvsend.at[h, d, w], recv_sem=kvrecv.at[h, slot],
            device_id=dev(2 * (chip + d) + to, sec), device_id_type=MESH,
        )

    def kv_half(h, w):
        to = lax.rem(core + w, 2)
        return pltpu.make_async_remote_copy(
            src_ref=kv_ref.at[half, :, cols(to * heads + h, HD)], dst_ref=kvbuf.at[h, half, core],
            send_sem=kvsend.at[h, depth, w], recv_sem=kvrecv.at[h, core],
            device_id=dev(2 * (chip + depth) + to, sec), device_id_type=MESH,
        )

    def kv_wait(h, slot):
        return pltpu.make_async_remote_copy(
            src_ref=kv_ref.at[:, :, pl.ds(0, HD)], dst_ref=kvbuf.at[h, :, slot],
            send_sem=kvsend.at[h, 0, 0], recv_sem=kvrecv.at[h, slot],
            device_id=dev(2 * chip + other, sec), device_id_type=MESH,
        )

    def half_wait(h, slot):
        return pltpu.make_async_remote_copy(
            src_ref=kv_ref.at[half, :, pl.ds(0, HD)], dst_ref=kvbuf.at[h, half, slot],
            send_sem=kvsend.at[h, 0, 0], recv_sem=kvrecv.at[h, slot],
            device_id=dev(2 * chip + other, sec), device_id_type=MESH,
        )

    def forward_copy(h, part):
        return pltpu.make_async_remote_copy(
            src_ref=kvbuf.at[h, part, pl.ds(0, 2)], dst_ref=kvbuf.at[h, part, pl.ds(0, 2)],
            send_sem=fsend.at[h], recv_sem=frecv.at[h],
            device_id=dev(me, mate), device_id_type=MESH,
        )

    def far_sends(h, act):
        @pl.when(chip + depth < chips)
        def _():
            if paired:
                @pl.when(place >= 1)
                def _():
                    for w in range(2):
                        act(kv_half(h, w))

                @pl.when(place < 1)
                def _():
                    for w in range(2):
                        act(kv_copy(h, depth, w))
            else:
                for w in range(2):
                    act(kv_copy(h, depth, w))

    def near_sends(h, act):
        for d in range(depth - 1, 0, -1):
            @pl.when(chip + d < chips)
            def _():
                for w in range(2):
                    act(kv_copy(h, d, w))

    def start(copy):
        copy.start()

    def wait_send(copy):
        copy.wait_send()

    def forward(h):
        if paired:
            @pl.when((place >= 1) & (chip >= depth))
            def _():
                for slot in range(2):
                    half_wait(h, slot).wait_recv()
                forward_copy(h, half).start()

    def kv_arrival(h, pair):
        if pair > 0:
            @pl.when(chip >= depth - pair)
            def _():
                for slot in (2 * pair, 2 * pair + 1):
                    kv_wait(h, slot).wait_recv()

            return

        @pl.when(chip >= depth)
        def _():
            if paired:
                @pl.when(place >= 1)
                def _():
                    forward_copy(h, 1 - half).wait_recv()

                @pl.when(place < 1)
                def _():
                    for slot in range(2):
                        kv_wait(h, slot).wait_recv()
            else:
                for slot in range(2):
                    kv_wait(h, slot).wait_recv()

    def x_copy(h, pair, t, k):
        to = lax.rem(sec + t, sections)
        return pltpu.make_async_remote_copy(
            src_ref=sbuf.at[h, k, pl.ds(2 * pair, 2), pl.ds(pl.multiple_of(to * piece, piece), piece)],
            dst_ref=xbuf.at[h, t - 1, k, pl.ds(2 * pair, 2)],
            send_sem=xsend.at[h, pair, t - 1, k], recv_sem=xrecv.at[h, pair, t - 1, k],
            device_id=dev(me, to), device_id_type=MESH,
        )

    def u_copy(h, k):
        return pltpu.make_async_remote_copy(
            src_ref=sbuf.at[h, k, pl.ds(reach - 2, 2)], dst_ref=ubuf.at[h, k],
            send_sem=usend.at[h, k], recv_sem=urecv.at[h, k],
            device_id=dev(2 * (chip - 1) + core, sec), device_id_type=MESH,
        )

    def g_copy(h, k, slot):
        d = (reach + 1 - slot) // 2
        return pltpu.make_async_remote_copy(
            src_ref=tbuf.at[h, slot, k], dst_ref=rbuf.at[d, core, h, k],
            send_sem=gsend.at[h, slot, k], recv_sem=grecv.at[d, core, h, k],
            device_id=dev(2 * (chip - d) + (slot - reach) % 2, sec), device_id_type=MESH,
        )

    def g_wait(h, k, d, c):
        return pltpu.make_async_remote_copy(
            src_ref=tbuf.at[h, 0, k], dst_ref=rbuf.at[d, c, h, k],
            send_sem=gsend.at[h, 0, k], recv_sem=grecv.at[d, c, h, k],
            device_id=dev(2 * chip + other, sec), device_id_type=MESH,
        )

    def when_pair(pair, run):
        if pair < depth:
            pl.when(chip >= depth - pair)(run)
        else:
            run()

    def when_sent(slot, run):
        if slot < reach:
            run()
        else:
            pl.when(core != slot - reach)(run)

    def scatter(h, k, pairs):
        def send(pair):
            for t in range(1, sections):
                x_copy(h, pair, t, k).start()

        for pair in pairs:
            when_pair(pair, functools.partial(send, pair))

    def deliver(h, k, pairs):
        own = pl.ds(pl.multiple_of(sec * piece, piece), piece)

        def run(pair):
            for t in range(1, sections):
                x_copy(h, pair, t, k).wait_recv()
            for slot in (2 * pair, 2 * pair + 1):
                total = sbuf[h, k, slot, own].astype(jnp.float32)
                for t in range(1, sections):
                    total = total + xbuf[h, t - 1, k, slot].astype(jnp.float32)
                tbuf[h, slot, k] = total.astype(jnp.bfloat16)
                when_sent(slot, lambda: g_copy(h, k, slot).start())

        for pair in pairs:
            when_pair(pair, functools.partial(run, pair))

    def dq_copy(h):
        return pltpu.make_async_remote_copy(
            src_ref=dqbuf.at[h, other], dst_ref=dq_ref.at[:, cols(core * heads + h, gw)],
            send_sem=dqsend.at[h], recv_sem=dqrecv.at[h],
            device_id=dev(2 * chip + other, sec), device_id_type=MESH,
        )

    def dq_wait(h):
        return pltpu.make_async_remote_copy(
            src_ref=dqbuf.at[h, other], dst_ref=dq_ref.at[:, cols(other * heads + h, gw)],
            send_sem=dqsend.at[h], recv_sem=dqrecv.at[h],
            device_id=dev(2 * chip + other, sec), device_id_type=MESH,
        )

    def dq_local(h):
        return pltpu.make_async_copy(
            dqbuf.at[h, core], dq_ref.at[:, cols(core * heads + h, gw)], dqloc.at[h]
        )

    barrier = pltpu.get_barrier_semaphore()

    def greet(ctx, section):
        pl.semaphore_signal(barrier, inc=1, device_id=dev(ctx, section), device_id_type=MESH)

    for t in range(1, sections):
        greet(me, lax.rem(sec + t, sections))
    for step in range(-depth, depth + 1):
        @pl.when((chip + step >= 0) & (chip + step < chips))
        def _():
            for w in range(2):
                if step == 0 and w == 0:
                    continue
                greet(2 * (chip + step) + lax.rem(core + w, 2), sec)

    docs_copy = pltpu.make_async_copy(docs_ref, docs, docsem)
    docs_copy.start()
    for h in range(heads):
        for copy in local_copies(h):
            copy.start()

    near = jnp.minimum(chip, depth) + jnp.minimum(chips - 1 - chip, depth)
    pl.semaphore_wait(barrier, 2 * near + 1 + sections - 1)

    far_sends(0, start)
    near_sends(0, start)
    for h in range(heads):
        kv_copy(h, 0, 1).start()
        for copy in q_copies(h):
            copy.start()

    for d in range(1, depth + 1):
        @pl.when(chip - d < 0)
        def _():
            for slot in (reach - 2 * d, reach - 2 * d + 1):
                for h in range(heads):
                    kvbuf[h, :, slot] = jnp.zeros((2, rows, HD), jnp.bfloat16)

        @pl.when(chip + d >= chips)
        def _():
            rbuf[d] = jnp.zeros(rbuf.shape[1:], jnp.bfloat16)

    for h in range(heads):
        dsbuf[h, 0:rows, width : 2 * width] = jnp.zeros((rows, width), jnp.bfloat16)
        dsbuf[h, (reach + 1) * rows : blocks * rows, 0:width] = jnp.zeros((rows, width), jnp.bfloat16)
    docs_copy.wait()
    row_at = lax.broadcasted_iota(jnp.int32, (rows, rows), 0)
    col_at = lax.broadcasted_iota(jnp.int32, (rows, rows), 1)
    for slot in range(blocks):
        at = 2 * chip - reach + slot
        kdoc = docs[pl.ds(jnp.maximum(at, 0), 1), :].astype(jnp.float32)
        kdoc = jnp.transpose(jnp.broadcast_to(kdoc, (rows, rows)))
        for sub in range(2):
            if not 0 <= slot - sub <= reach:
                continue
            qdoc = docs[pl.ds(2 * chip + sub, 1), :].astype(jnp.float32)
            kplace = at * rows + row_at
            qplace = (2 * chip + sub) * rows + col_at
            seen = (kplace <= qplace) & (kplace >= 0) & (kdoc == qdoc)
            bias[sub, (slot - sub) * rows : (slot - sub + 1) * rows] = jnp.where(seen, 0.0, NEG)

    def stacked(h, k, sub):
        buf = (qbuf, dobuf)[k]
        return jnp.concatenate([buf[h, sub, :, i * HD : (i + 1) * HD] for i in range(group)], axis=0)

    def part_rows(sub, part):
        if part == 0:
            return slice((reach - sub) * rows, window)
        return slice(max(2 * part - 2 - sub, 0) * rows, (2 * part - sub) * rows)

    def score_part(h, sub, part):
        at = part_rows(sub, part)
        slots = slice(at.start // rows + sub, at.stop // rows + sub)
        k = kvbuf[h, 0, slots].reshape(at.stop - at.start, HD)
        v = kvbuf[h, 1, slots].reshape(at.stop - at.start, HD)
        nt = (((1,), (1,)), ((), ()))
        s = lax.dot_general(k, stacked(h, 0, sub), nt, preferred_element_type=jnp.float32)
        dp = lax.dot_general(v, stacked(h, 1, sub), nt, preferred_element_type=jnp.float32)
        s = s * (scale * LOG2E) + jnp.concatenate([bias[sub, at]] * (layers * group), axis=1)
        top = jnp.max(s, axis=0, keepdims=True)
        e = jnp.exp2(s - top)
        ebuf[h, sub, at] = e
        dpbuf[h, sub, at] = dp
        stat[h, sub, part, 0:1] = top
        stat[h, sub, part, 1:2] = jnp.sum(e, axis=0, keepdims=True)
        stat[h, sub, part, 2:3] = jnp.sum(e * dp, axis=0, keepdims=True)

    def prob_part(h, sub):
        parts = range(depth + 1)
        tops = [stat[h, sub, part, 0:1] for part in parts]
        top = functools.reduce(jnp.maximum, tops)
        factors = [jnp.exp2(t - top) for t in tops]
        inverse = 1.0 / sum(factors[part] * stat[h, sub, part, 1:2] for part in parts)
        factors = [f * inverse for f in factors]
        delta = sum(factors[part] * stat[h, sub, part, 2:3] for part in parts)
        for part in parts:
            at = part_rows(sub, part)
            keys_at = slice(at.start + sub * rows, at.stop + sub * rows)
            for i in range(group):
                span = slice(i * layers * rows, (i + 1) * layers * rows)
                p = ebuf[h, sub, at, span] * factors[part][:, span]
                ds = p * (dpbuf[h, sub, at, span] - delta[:, span])
                to = slice(sub * width + span.start, sub * width + span.stop)
                pbuf[keys_at, to] = p.astype(jnp.bfloat16)
                dsbuf[h, keys_at, to] = ds.astype(jnp.bfloat16)

    def key_part(h, k):
        stack = jnp.concatenate([stacked(h, k, sub) for sub in range(2)], axis=0)
        at = slice(rows, (reach + 1) * rows)
        total = jnp.dot(dsbuf[h, at] if k == 0 else pbuf[at], stack, preferred_element_type=jnp.float32)
        total = total * scale if k == 0 else total
        sbuf[h, k, 1 : reach + 1] = total.astype(jnp.bfloat16).reshape(reach, rows, HD)

    def edge_part(h, k, slot, sub):
        at = slice(slot * rows, (slot + 1) * rows)
        to = slice(sub * width, (sub + 1) * width)
        weights = dsbuf[h, at, to] if k == 0 else pbuf[at, to]
        total = jnp.dot(weights, stacked(h, k, sub), preferred_element_type=jnp.float32)
        sbuf[h, k, slot] = (total * scale if k == 0 else total).astype(jnp.bfloat16)

    def query_part(h, sub):
        kt = jnp.transpose(kvbuf[h, 0].reshape(blocks * rows, HD))
        to = pl.ds(pl.multiple_of(sub * width, rows), width)
        dqt = jnp.dot(kt, dsbuf[h, :, to], preferred_element_type=jnp.float32) * scale
        for i in range(group):
            dqbuf[h, sub, :, i * HD : (i + 1) * HD] = jnp.transpose(
                dqt[:, i * layers * rows : (i + 1) * layers * rows]
            ).astype(jnp.bfloat16)

    def own_scores(h, unused):
        for copy in local_copies(h):
            copy.wait()
        for copy in q_copies(h):
            copy.wait_recv()
        for c in range(2):
            pl.when(core != c)(lambda: kv_wait(h, reach + c).wait_recv())
        for sub in range(2):
            score_part(h, sub, 0)
        return unused

    lax.fori_loop(0, heads, own_scores, 0)

    forward(0)
    for h in range(1, heads):
        far_sends(h - 1, wait_send)
        far_sends(h, start)
        near_sends(h - 1, wait_send)
        near_sends(h, start)

    last = heads - 1

    def head_step(h, unused):
        def scores(order):
            for pair in order:
                kv_arrival(h, pair)
                if pair == 0:
                    pl.when(h + 1 < heads)(lambda: forward(h + 1))
                for sub in range(2):
                    score_part(h, sub, pair + 1)

        pl.when(place < 1)(lambda: scores(range(depth)))
        pl.when(place >= 1)(lambda: scores(range(depth - 1, -1, -1)))
        prob_part(h, 0)
        prob_part(h, 1)
        for k in (1, 0):
            pl.when(h > 0)(lambda: deliver(h - 1, k, range(depth - 1)))
            key_part(h, k)
            edge_part(h, k, 0, 0)
            scatter(h, k, range(depth - 1))
            pl.when(h == last)(lambda: scatter(h, k, range(depth - 1, depth)))
            pl.when((h < last) & (chip >= 1))(lambda: u_copy(h, k).start())
        for k in (1, 0):
            edge_part(h, k, reach + 1, 1)
        return unused

    far, near = range(depth), range(depth, depth + 1)
    lax.fori_loop(0, heads, head_step, 0)
    for h in range(heads):
        for k in (1, 0):
            if h < last:
                @pl.when(chip + 1 < chips)
                def _():
                    u_copy(h, k).wait_recv()
                    own = sbuf[h, k, reach:blocks].astype(jnp.float32) + ubuf[h, k].astype(jnp.float32)
                    sbuf[h, k, reach:blocks] = own.astype(jnp.bfloat16)

            scatter(h, k, near)

    def queries(h):
        query_part(h, other)
        dq_copy(h).start()
        query_part(h, core)
        dq_local(h).start()

    for h in range(last):
        queries(h)
    deliver(last, 1, far)
    queries(last)
    deliver(last, 0, far)

    def own_step(h, unused):
        for k in (1, 0):
            deliver(h, k, near)
            rbuf[0, core, h, k] = tbuf[h, reach + core, k]
        return unused

    lax.fori_loop(0, heads, own_step, 0)

    for h in range(heads):
        steps = [d for d in range(depth, 0, -1) if d > 1 or h == last]
        for k in (1, 0):
            for c in range(2):
                for d in steps + [0]:
                    pl.when(core != c if d == 0 else chip + d < chips)(lambda: g_wait(h, k, d, c).wait_recv())
                total = rbuf[0, c, h, k].astype(jnp.float32)
                for d in steps:
                    total = total + rbuf[d, c, h, k].astype(jnp.float32)
                g = c * heads + h
                out_ref[k, :, g * HD : (g + 1) * HD] = total.astype(jnp.bfloat16)

    def finish(h):
        dq_wait(h).wait_recv()
        dq_copy(h).wait_send()
        dq_local(h).wait()
        for copy in q_copies(h):
            copy.wait_send()
        kv_copy(h, 0, 1).wait_send()
        if h == last:
            far_sends(h, wait_send)
            near_sends(h, wait_send)
        if paired:
            @pl.when((place >= 1) & (chip >= depth))
            def _():
                forward_copy(h, half).wait_send()

        def sent(pair):
            for t in range(1, sections):
                for k in range(2):
                    x_copy(h, pair, t, k).wait_send()
            for slot in (2 * pair, 2 * pair + 1):
                for k in range(2):
                    when_sent(slot, lambda: g_copy(h, k, slot).wait_send())

        for pair in range(depth + 1):
            if pair == depth - 1 and h < last:
                @pl.when(chip >= 1)
                def _():
                    for k in range(2):
                        u_copy(h, k).wait_send()
            else:
                when_pair(pair, functools.partial(sent, pair))

    for h in range(heads):
        finish(h)


def body(queries, grad_out, keys_values, doc_ids):
    layers, rows, width = queries.shape
    kv_width = keys_values.shape[2]
    heads_kv = kv_width // HD
    group = width // kv_width
    n = lax.axis_size("ctx")
    sections = lax.axis_size("section")
    reach = n // 4
    heads = heads_kv // 2
    blocks = reach + 2
    window = (reach + 1) * rows
    piece = rows // sections
    depth = reach // 2
    bf, f32 = jnp.bfloat16, jnp.float32
    dma = pltpu.SemaphoreType.DMA
    hbm = pl.BlockSpec(memory_space=pl.ANY)
    vmem = pl.BlockSpec(memory_space=pltpu.VMEM)
    grad_queries, grad_kv = pl.pallas_call(
        functools.partial(kernel, n, sections, reach, heads_kv, group),
        out_shape=(
            jax.ShapeDtypeStruct((layers * rows, width), bf),
            jax.ShapeDtypeStruct((2, piece, kv_width), bf),
        ),
        in_specs=[hbm, hbm, hbm, hbm],
        out_specs=(hbm, vmem),
        scratch_shapes=[
            pltpu.VMEM((n, rows), jnp.int32),
            pltpu.VMEM((heads, 2, layers * rows, group * HD), bf),
            pltpu.VMEM((heads, 2, layers * rows, group * HD), bf),
            pltpu.VMEM((heads, 2, blocks, rows, HD), bf),
            pltpu.VMEM((2, window, rows), f32),
            pltpu.VMEM((heads, 2, window, group * layers * rows), f32),
            pltpu.VMEM((heads, 2, window, group * layers * rows), f32),
            pltpu.VMEM((heads, 2, depth + 1, 8, group * layers * rows), f32),
            pltpu.VMEM((blocks * rows, 2 * group * layers * rows), bf),
            pltpu.VMEM((heads, blocks * rows, 2 * group * layers * rows), bf),
            pltpu.VMEM((heads, 2, blocks, rows, HD), bf),
            pltpu.VMEM((heads, 2, 2, rows, HD), bf),
            pltpu.VMEM((heads, max(sections - 1, 1), 2, blocks, piece, HD), bf),
            pltpu.VMEM((heads, blocks, 2, piece, HD), bf),
            pltpu.VMEM((depth + 1, 2, heads, 2, piece, HD), bf),
            pltpu.VMEM((heads, 2, layers * rows, group * HD), bf),
            dma,
            dma((heads, 3)),
            dma((heads, 2)),
            dma((heads, 2)),
            dma((heads, depth + 1, 2)),
            dma((heads, blocks)),
            dma((heads,)),
            dma((heads,)),
            dma((heads, 2)),
            dma((heads, 2)),
            dma((heads, depth + 1, max(sections - 1, 1), 2)),
            dma((heads, depth + 1, max(sections - 1, 1), 2)),
            dma((heads, blocks, 2)),
            dma((depth + 1, 2, heads, 2)),
            dma((heads,)),
            dma((heads,)),
            dma((heads,)),
        ],
        compiler_params=pltpu.CompilerParams(
            collective_id=0, has_side_effects=True, vmem_limit_bytes=(24 + 4 * reach) * 1024 * 1024
        ),
        name="cross_backward",
    )(
        *[
            pltpu.with_memory_space_constraint(x, pltpu.HBM)
            for x in (
                queries.reshape(layers * rows, width), grad_out.reshape(layers * rows, width),
                keys_values, doc_ids.reshape(n, rows),
            )
        ]
    )
    return grad_queries.reshape(queries.shape), grad_kv


def solution(mesh):
    return jax.shard_map(
        body,
        mesh=mesh,
        in_specs=(P("section", "ctx", None), P("section", "ctx", None), P(None, "ctx", None), P()),
        out_specs=(P("section", "ctx", None), P(None, ("ctx", "section"), None)),
        check_vma=False,
    )
```

```python
import functools

import jax
import jax.numpy as jnp
from jax import lax
from jax.experimental import pallas as pl
from jax.experimental.pallas import tpu as pltpu
from jax.sharding import PartitionSpec as P

HD = 128
MESH = pl.DeviceIdType.MESH
LOG2E = 1.4426950408889634
NEG = -1e30


def kernel(
    n, sections, reach, heads_kv, group,
    q_ref, do_ref, kv_ref, docs_ref,
    dq_ref, out_ref,
    docs, qbuf, dobuf, kvbuf, bias, ebuf, dpbuf, stat, pbuf, dsbuf, sbuf, ubuf, xbuf, tbuf, rbuf, dqbuf,
    docsem, lsem, qsend, qrecv, kvsend, kvrecv, fsend, frecv, usend, urecv, xsend, xrecv, gsend, grecv, dqsend, dqrecv, dqloc,
):
    me = lax.axis_index("ctx")
    sec = lax.axis_index("section")
    rows = kv_ref.shape[1]
    layers = q_ref.shape[0] // rows
    width = group * layers * rows
    core = lax.rem(me, 2)
    other = 1 - core
    chip = me // 2
    chips = n // 2
    depth = reach // 2
    place = lax.rem(chip, depth)
    blocks = reach + 2
    heads = heads_kv // 2
    gw = group * HD
    window = (reach + 1) * rows
    piece = rows // sections
    scale = HD ** (-0.5)
    paired = sections % 2 == 0
    half = lax.rem(sec, 2)
    mate = sec + 1 - 2 * half

    def dev(ctx, section):
        return {"ctx": ctx, "section": section}

    def cols(head, width):
        return pl.ds(pl.multiple_of(head * width, HD), width)

    def local_copies(h):
        g = core * heads + h
        return [
            pltpu.make_async_copy(q_ref.at[:, cols(g, gw)], qbuf.at[h, core], lsem.at[h, 0]),
            pltpu.make_async_copy(do_ref.at[:, cols(g, gw)], dobuf.at[h, core], lsem.at[h, 1]),
            pltpu.make_async_copy(
                kv_ref.at[:, :, cols(g, HD)], kvbuf.at[h, :, reach + core], lsem.at[h, 2]
            ),
        ]

    def q_copies(h):
        g = other * heads + h
        partner = dev(2 * chip + other, sec)
        return [
            pltpu.make_async_remote_copy(
                src_ref=src.at[:, cols(g, gw)], dst_ref=dst.at[h, core],
                send_sem=qsend.at[h, k], recv_sem=qrecv.at[h, k],
                device_id=partner, device_id_type=MESH,
            )
            for k, (src, dst) in enumerate([(q_ref, qbuf), (do_ref, dobuf)])
        ]

    def kv_copy(h, d, w):
        to = lax.rem(core + w, 2)
        slot = core - 2 * d + reach
        return pltpu.make_async_remote_copy(
            src_ref=kv_ref.at[:, :, cols(to * heads + h, HD)], dst_ref=kvbuf.at[h, :, slot],
            send_sem=kvsend.at[h, d, w], recv_sem=kvrecv.at[h, slot],
            device_id=dev(2 * (chip + d) + to, sec), device_id_type=MESH,
        )

    def kv_half(h, w):
        to = lax.rem(core + w, 2)
        return pltpu.make_async_remote_copy(
            src_ref=kv_ref.at[half, :, cols(to * heads + h, HD)], dst_ref=kvbuf.at[h, half, core],
            send_sem=kvsend.at[h, depth, w], recv_sem=kvrecv.at[h, core],
            device_id=dev(2 * (chip + depth) + to, sec), device_id_type=MESH,
        )

    def kv_wait(h, slot):
        return pltpu.make_async_remote_copy(
            src_ref=kv_ref.at[:, :, pl.ds(0, HD)], dst_ref=kvbuf.at[h, :, slot],
            send_sem=kvsend.at[h, 0, 0], recv_sem=kvrecv.at[h, slot],
            device_id=dev(2 * chip + other, sec), device_id_type=MESH,
        )

    def half_wait(h, slot):
        return pltpu.make_async_remote_copy(
            src_ref=kv_ref.at[half, :, pl.ds(0, HD)], dst_ref=kvbuf.at[h, half, slot],
            send_sem=kvsend.at[h, 0, 0], recv_sem=kvrecv.at[h, slot],
            device_id=dev(2 * chip + other, sec), device_id_type=MESH,
        )

    def forward_copy(h, part):
        return pltpu.make_async_remote_copy(
            src_ref=kvbuf.at[h, part, pl.ds(0, 2)], dst_ref=kvbuf.at[h, part, pl.ds(0, 2)],
            send_sem=fsend.at[h], recv_sem=frecv.at[h],
            device_id=dev(me, mate), device_id_type=MESH,
        )

    def far_sends(h, act):
        @pl.when(chip + depth < chips)
        def _():
            if paired:
                @pl.when(place >= 1)
                def _():
                    for w in range(2):
                        act(kv_half(h, w))

                @pl.when(place < 1)
                def _():
                    for w in range(2):
                        act(kv_copy(h, depth, w))
            else:
                for w in range(2):
                    act(kv_copy(h, depth, w))

    def near_sends(h, act):
        for d in range(depth - 1, 0, -1):
            @pl.when(chip + d < chips)
            def _():
                for w in range(2):
                    act(kv_copy(h, d, w))

    def start(copy):
        copy.start()

    def wait_send(copy):
        copy.wait_send()

    def forward(h):
        if paired:
            @pl.when((place >= 1) & (chip >= depth))
            def _():
                for slot in range(2):
                    half_wait(h, slot).wait_recv()
                forward_copy(h, half).start()

    def kv_arrival(h, pair):
        if pair > 0:
            @pl.when(chip >= depth - pair)
            def _():
                for slot in (2 * pair, 2 * pair + 1):
                    kv_wait(h, slot).wait_recv()

            return

        @pl.when(chip >= depth)
        def _():
            if paired:
                @pl.when(place >= 1)
                def _():
                    forward_copy(h, 1 - half).wait_recv()

                @pl.when(place < 1)
                def _():
                    for slot in range(2):
                        kv_wait(h, slot).wait_recv()
            else:
                for slot in range(2):
                    kv_wait(h, slot).wait_recv()

    def x_copy(h, pair, t, k):
        to = lax.rem(sec + t, sections)
        return pltpu.make_async_remote_copy(
            src_ref=sbuf.at[h, k, pl.ds(2 * pair, 2), pl.ds(pl.multiple_of(to * piece, piece), piece)],
            dst_ref=xbuf.at[h, t - 1, k, pl.ds(2 * pair, 2)],
            send_sem=xsend.at[h, pair, t - 1, k], recv_sem=xrecv.at[h, pair, t - 1, k],
            device_id=dev(me, to), device_id_type=MESH,
        )

    def u_copy(h):
        return pltpu.make_async_remote_copy(
            src_ref=sbuf.at[h, 1, pl.ds(reach - 2, 2)], dst_ref=ubuf.at[h],
            send_sem=usend.at[h], recv_sem=urecv.at[h],
            device_id=dev(2 * (chip - 1) + core, sec), device_id_type=MESH,
        )

    def g_copy(h, k, slot):
        d = (reach + 1 - slot) // 2
        return pltpu.make_async_remote_copy(
            src_ref=tbuf.at[h, slot, k], dst_ref=rbuf.at[d, core, h, k],
            send_sem=gsend.at[h, slot, k], recv_sem=grecv.at[d, core, h, k],
            device_id=dev(2 * (chip - d) + (slot - reach) % 2, sec), device_id_type=MESH,
        )

    def g_wait(h, k, d, c):
        return pltpu.make_async_remote_copy(
            src_ref=tbuf.at[h, 0, k], dst_ref=rbuf.at[d, c, h, k],
            send_sem=gsend.at[h, 0, k], recv_sem=grecv.at[d, c, h, k],
            device_id=dev(2 * chip + other, sec), device_id_type=MESH,
        )

    def when_pair(pair, run):
        if pair < depth:
            pl.when(chip >= depth - pair)(run)
        else:
            run()

    def when_sent(slot, run):
        if slot < reach:
            run()
        else:
            pl.when(core != slot - reach)(run)

    def scatter(h, k, pairs):
        def send(pair):
            for t in range(1, sections):
                x_copy(h, pair, t, k).start()

        for pair in pairs:
            when_pair(pair, functools.partial(send, pair))

    def deliver(h, k, pairs):
        own = pl.ds(pl.multiple_of(sec * piece, piece), piece)

        def run(pair):
            for t in range(1, sections):
                x_copy(h, pair, t, k).wait_recv()
            for slot in (2 * pair, 2 * pair + 1):
                total = sbuf[h, k, slot, own].astype(jnp.float32)
                for t in range(1, sections):
                    total = total + xbuf[h, t - 1, k, slot].astype(jnp.float32)
                tbuf[h, slot, k] = total.astype(jnp.bfloat16)
                when_sent(slot, lambda: g_copy(h, k, slot).start())

        for pair in pairs:
            when_pair(pair, functools.partial(run, pair))

    def dq_copy(h):
        return pltpu.make_async_remote_copy(
            src_ref=dqbuf.at[h, other], dst_ref=dq_ref.at[:, cols(core * heads + h, gw)],
            send_sem=dqsend.at[h], recv_sem=dqrecv.at[h],
            device_id=dev(2 * chip + other, sec), device_id_type=MESH,
        )

    def dq_wait(h):
        return pltpu.make_async_remote_copy(
            src_ref=dqbuf.at[h, other], dst_ref=dq_ref.at[:, cols(other * heads + h, gw)],
            send_sem=dqsend.at[h], recv_sem=dqrecv.at[h],
            device_id=dev(2 * chip + other, sec), device_id_type=MESH,
        )

    def dq_local(h):
        return pltpu.make_async_copy(
            dqbuf.at[h, core], dq_ref.at[:, cols(core * heads + h, gw)], dqloc.at[h]
        )

    barrier = pltpu.get_barrier_semaphore()

    def greet(ctx, section):
        pl.semaphore_signal(barrier, inc=1, device_id=dev(ctx, section), device_id_type=MESH)

    for t in range(1, sections):
        greet(me, lax.rem(sec + t, sections))
    for step in range(-depth, depth + 1):
        @pl.when((chip + step >= 0) & (chip + step < chips))
        def _():
            for w in range(2):
                if step == 0 and w == 0:
                    continue
                greet(2 * (chip + step) + lax.rem(core + w, 2), sec)

    docs_copy = pltpu.make_async_copy(docs_ref, docs, docsem)
    docs_copy.start()
    for h in range(heads):
        for copy in local_copies(h):
            copy.start()

    near = jnp.minimum(chip, depth) + jnp.minimum(chips - 1 - chip, depth)
    pl.semaphore_wait(barrier, 2 * near + 1 + sections - 1)

    far_sends(0, start)
    near_sends(0, start)
    for h in range(heads):
        kv_copy(h, 0, 1).start()
        for copy in q_copies(h):
            copy.start()

    for d in range(1, depth + 1):
        @pl.when(chip - d < 0)
        def _():
            for slot in (reach - 2 * d, reach - 2 * d + 1):
                for h in range(heads):
                    kvbuf[h, :, slot] = jnp.zeros((2, rows, HD), jnp.bfloat16)

        @pl.when(chip + d >= chips)
        def _():
            rbuf[d] = jnp.zeros(rbuf.shape[1:], jnp.bfloat16)

    for h in range(heads):
        dsbuf[h, 0:rows, width : 2 * width] = jnp.zeros((rows, width), jnp.bfloat16)
        dsbuf[h, (reach + 1) * rows : blocks * rows, 0:width] = jnp.zeros((rows, width), jnp.bfloat16)
    docs_copy.wait()
    row_at = lax.broadcasted_iota(jnp.int32, (rows, rows), 0)
    col_at = lax.broadcasted_iota(jnp.int32, (rows, rows), 1)
    for slot in range(blocks):
        at = 2 * chip - reach + slot
        kdoc = docs[pl.ds(jnp.maximum(at, 0), 1), :].astype(jnp.float32)
        kdoc = jnp.transpose(jnp.broadcast_to(kdoc, (rows, rows)))
        for sub in range(2):
            if not 0 <= slot - sub <= reach:
                continue
            qdoc = docs[pl.ds(2 * chip + sub, 1), :].astype(jnp.float32)
            kplace = at * rows + row_at
            qplace = (2 * chip + sub) * rows + col_at
            seen = (kplace <= qplace) & (kplace >= 0) & (kdoc == qdoc)
            bias[sub, (slot - sub) * rows : (slot - sub + 1) * rows] = jnp.where(seen, 0.0, NEG)

    def stacked(h, k, sub):
        buf = (qbuf, dobuf)[k]
        return jnp.concatenate([buf[h, sub, :, i * HD : (i + 1) * HD] for i in range(group)], axis=0)

    def part_rows(sub, part):
        if part == 0:
            return slice((reach - sub) * rows, window)
        return slice(max(2 * part - 2 - sub, 0) * rows, (2 * part - sub) * rows)

    def score_part(h, sub, part):
        at = part_rows(sub, part)
        slots = slice(at.start // rows + sub, at.stop // rows + sub)
        k = kvbuf[h, 0, slots].reshape(at.stop - at.start, HD)
        v = kvbuf[h, 1, slots].reshape(at.stop - at.start, HD)
        nt = (((1,), (1,)), ((), ()))
        s = lax.dot_general(k, stacked(h, 0, sub), nt, preferred_element_type=jnp.float32)
        dp = lax.dot_general(v, stacked(h, 1, sub), nt, preferred_element_type=jnp.float32)
        s = s * (scale * LOG2E) + jnp.concatenate([bias[sub, at]] * (layers * group), axis=1)
        top = jnp.max(s, axis=0, keepdims=True)
        e = jnp.exp2(s - top)
        ebuf[h, sub, at] = e
        dpbuf[h, sub, at] = dp
        stat[h, sub, part, 0:1] = top
        stat[h, sub, part, 1:2] = jnp.sum(e, axis=0, keepdims=True)
        stat[h, sub, part, 2:3] = jnp.sum(e * dp, axis=0, keepdims=True)

    def prob_part(h, sub):
        parts = range(depth + 1)
        tops = [stat[h, sub, part, 0:1] for part in parts]
        top = functools.reduce(jnp.maximum, tops)
        factors = [jnp.exp2(t - top) for t in tops]
        inverse = 1.0 / sum(factors[part] * stat[h, sub, part, 1:2] for part in parts)
        factors = [f * inverse for f in factors]
        delta = sum(factors[part] * stat[h, sub, part, 2:3] for part in parts)
        for part in parts:
            at = part_rows(sub, part)
            keys_at = slice(at.start + sub * rows, at.stop + sub * rows)
            for i in range(group):
                span = slice(i * layers * rows, (i + 1) * layers * rows)
                p = ebuf[h, sub, at, span] * factors[part][:, span]
                ds = p * (dpbuf[h, sub, at, span] - delta[:, span])
                to = slice(sub * width + span.start, sub * width + span.stop)
                pbuf[keys_at, to] = p.astype(jnp.bfloat16)
                dsbuf[h, keys_at, to] = ds.astype(jnp.bfloat16)

    def key_part(h, k):
        stack = jnp.concatenate([stacked(h, k, sub) for sub in range(2)], axis=0)
        at = slice(rows, (reach + 1) * rows)
        total = jnp.dot(dsbuf[h, at] if k == 0 else pbuf[at], stack, preferred_element_type=jnp.float32)
        total = total * scale if k == 0 else total
        sbuf[h, k, 1 : reach + 1] = total.astype(jnp.bfloat16).reshape(reach, rows, HD)

    def edge_part(h, k, slot, sub):
        at = slice(slot * rows, (slot + 1) * rows)
        to = slice(sub * width, (sub + 1) * width)
        weights = dsbuf[h, at, to] if k == 0 else pbuf[at, to]
        total = jnp.dot(weights, stacked(h, k, sub), preferred_element_type=jnp.float32)
        sbuf[h, k, slot] = (total * scale if k == 0 else total).astype(jnp.bfloat16)

    def query_part(h, sub):
        kt = jnp.transpose(kvbuf[h, 0].reshape(blocks * rows, HD))
        to = pl.ds(pl.multiple_of(sub * width, rows), width)
        dqt = jnp.dot(kt, dsbuf[h, :, to], preferred_element_type=jnp.float32) * scale
        for i in range(group):
            dqbuf[h, sub, :, i * HD : (i + 1) * HD] = jnp.transpose(
                dqt[:, i * layers * rows : (i + 1) * layers * rows]
            ).astype(jnp.bfloat16)

    def own_scores(h, unused):
        for copy in local_copies(h):
            copy.wait()
        for copy in q_copies(h):
            copy.wait_recv()
        for c in range(2):
            pl.when(core != c)(lambda: kv_wait(h, reach + c).wait_recv())
        for sub in range(2):
            score_part(h, sub, 0)
        return unused

    own_scores(0, 0)
    forward(0)
    for h in range(1, heads):
        far_sends(h - 1, wait_send)
        far_sends(h, start)
        near_sends(h - 1, wait_send)
        near_sends(h, start)
        own_scores(h, 0)

    last = heads - 1
    far, near = range(depth), range(depth, depth + 1)

    def head_step(h, unused):
        def scores(order):
            for pair in order:
                kv_arrival(h, pair)
                if pair == 0:
                    pl.when(h + 1 < heads)(lambda: forward(h + 1))
                for sub in range(2):
                    score_part(h, sub, pair + 1)

        pl.when(place < 1)(lambda: scores(range(depth)))
        pl.when(place >= 1)(lambda: scores(range(depth - 1, -1, -1)))
        prob_part(h, 0)
        prob_part(h, 1)
        for k in (1, 0):
            pl.when(h > 0)(lambda: deliver(h - 1, k, range(depth - k)))
            key_part(h, k)
            edge_part(h, k, 0, 0)
            scatter(h, k, range(depth - 1))
            if k == 1:
                pl.when(h == last)(lambda: scatter(h, k, range(depth - 1, depth)))
                pl.when((h < last) & (chip >= 1))(lambda: u_copy(h).start())
            else:
                scatter(h, k, range(depth - 1, depth))
        for k in (0, 1):
            edge_part(h, k, reach + 1, 1)
            if k == 0:
                pl.when(h < last)(lambda: scatter(h, k, near))
        return unused

    lax.fori_loop(0, heads, head_step, 0)
    for h in range(heads):
        if h < last:
            @pl.when(chip + 1 < chips)
            def _():
                u_copy(h).wait_recv()
                own = sbuf[h, 1, reach:blocks].astype(jnp.float32) + ubuf[h].astype(jnp.float32)
                sbuf[h, 1, reach:blocks] = own.astype(jnp.bfloat16)

        scatter(h, 1, near)
    scatter(last, 0, near)

    def queries(h):
        query_part(h, other)
        dq_copy(h).start()
        query_part(h, core)
        dq_local(h).start()

    for h in range(last):
        queries(h)
    deliver(last, 1, far)
    query_part(last, other)
    dq_copy(last).start()
    deliver(last, 0, far)
    query_part(last, core)
    dq_local(last).start()

    def own_step(h, unused):
        for k in (1, 0):
            deliver(h, k, near)
            rbuf[0, core, h, k] = tbuf[h, reach + core, k]
        return unused

    lax.fori_loop(0, heads, own_step, 0)

    def collect(h, k):
        steps = [d for d in range(depth, 0, -1) if d > 1 or h == last or k == 0]
        for c in range(2):
            for d in steps + [0]:
                pl.when(core != c if d == 0 else chip + d < chips)(lambda: g_wait(h, k, d, c).wait_recv())
            total = rbuf[0, c, h, k].astype(jnp.float32)
            for d in steps:
                total = total + rbuf[d, c, h, k].astype(jnp.float32)
            g = c * heads + h
            out_ref[k, :, g * HD : (g + 1) * HD] = total.astype(jnp.bfloat16)

    for h in range(heads):
        for k in (1, 0):
            if h < last or k == 1:
                collect(h, k)

    def finish(h):
        dq_wait(h).wait_recv()
        dq_copy(h).wait_send()
        dq_local(h).wait()
        for copy in q_copies(h):
            copy.wait_send()
        kv_copy(h, 0, 1).wait_send()
        if h == last:
            far_sends(h, wait_send)
            near_sends(h, wait_send)
        if paired:
            @pl.when((place >= 1) & (chip >= depth))
            def _():
                forward_copy(h, half).wait_send()

        def sent(pair, k):
            for t in range(1, sections):
                x_copy(h, pair, t, k).wait_send()
            for slot in (2 * pair, 2 * pair + 1):
                when_sent(slot, lambda: g_copy(h, k, slot).wait_send())

        for pair in range(depth + 1):
            for k in range(2):
                if pair == depth - 1 and h < last and k == 1:
                    pl.when(chip >= 1)(lambda: u_copy(h).wait_send())
                else:
                    when_pair(pair, functools.partial(sent, pair, k))

    for h in range(heads):
        finish(h)
    collect(last, 0)


def body(queries, grad_out, keys_values, doc_ids):
    layers, rows, width = queries.shape
    kv_width = keys_values.shape[2]
    heads_kv = kv_width // HD
    group = width // kv_width
    n = lax.axis_size("ctx")
    sections = lax.axis_size("section")
    reach = n // 4
    heads = heads_kv // 2
    blocks = reach + 2
    window = (reach + 1) * rows
    piece = rows // sections
    depth = reach // 2
    bf, f32 = jnp.bfloat16, jnp.float32
    dma = pltpu.SemaphoreType.DMA
    hbm = pl.BlockSpec(memory_space=pl.ANY)
    vmem = pl.BlockSpec(memory_space=pltpu.VMEM)
    grad_queries, grad_kv = pl.pallas_call(
        functools.partial(kernel, n, sections, reach, heads_kv, group),
        out_shape=(
            jax.ShapeDtypeStruct((layers * rows, width), bf),
            jax.ShapeDtypeStruct((2, piece, kv_width), bf),
        ),
        in_specs=[hbm, hbm, hbm, hbm],
        out_specs=(hbm, vmem),
        scratch_shapes=[
            pltpu.VMEM((n, rows), jnp.int32),
            pltpu.VMEM((heads, 2, layers * rows, group * HD), bf),
            pltpu.VMEM((heads, 2, layers * rows, group * HD), bf),
            pltpu.VMEM((heads, 2, blocks, rows, HD), bf),
            pltpu.VMEM((2, window, rows), f32),
            pltpu.VMEM((heads, 2, window, group * layers * rows), f32),
            pltpu.VMEM((heads, 2, window, group * layers * rows), f32),
            pltpu.VMEM((heads, 2, depth + 1, 8, group * layers * rows), f32),
            pltpu.VMEM((blocks * rows, 2 * group * layers * rows), bf),
            pltpu.VMEM((heads, blocks * rows, 2 * group * layers * rows), bf),
            pltpu.VMEM((heads, 2, blocks, rows, HD), bf),
            pltpu.VMEM((heads, 2, rows, HD), bf),
            pltpu.VMEM((heads, max(sections - 1, 1), 2, blocks, piece, HD), bf),
            pltpu.VMEM((heads, blocks, 2, piece, HD), bf),
            pltpu.VMEM((depth + 1, 2, heads, 2, piece, HD), bf),
            pltpu.VMEM((heads, 2, layers * rows, group * HD), bf),
            dma,
            dma((heads, 3)),
            dma((heads, 2)),
            dma((heads, 2)),
            dma((heads, depth + 1, 2)),
            dma((heads, blocks)),
            dma((heads,)),
            dma((heads,)),
            dma((heads,)),
            dma((heads,)),
            dma((heads, depth + 1, max(sections - 1, 1), 2)),
            dma((heads, depth + 1, max(sections - 1, 1), 2)),
            dma((heads, blocks, 2)),
            dma((depth + 1, 2, heads, 2)),
            dma((heads,)),
            dma((heads,)),
            dma((heads,)),
        ],
        compiler_params=pltpu.CompilerParams(
            collective_id=0, has_side_effects=True, vmem_limit_bytes=(24 + 4 * reach) * 1024 * 1024
        ),
        name="cross_backward",
    )(
        *[
            pltpu.with_memory_space_constraint(x, pltpu.HBM)
            for x in (
                queries.reshape(layers * rows, width), grad_out.reshape(layers * rows, width),
                keys_values, doc_ids.reshape(n, rows),
            )
        ]
    )
    return grad_queries.reshape(queries.shape), grad_kv


def solution(mesh):
    return jax.shard_map(
        body,
        mesh=mesh,
        in_specs=(P("section", "ctx", None), P("section", "ctx", None), P(None, "ctx", None), P()),
        out_specs=(P("section", "ctx", None), P(None, ("ctx", "section"), None)),
        check_vma=False,
    )
```

```python
import functools

import jax
import jax.numpy as jnp
from jax import lax
from jax.experimental import pallas as pl
from jax.experimental.pallas import tpu as pltpu
from jax.sharding import PartitionSpec as P

HD = 128
MESH = pl.DeviceIdType.MESH
LOG2E = 1.4426950408889634
NEG = -1e30


def kernel(
    n, sections, reach, heads_kv, group,
    q_ref, do_ref, kv_ref, docs_ref,
    dq_ref, out_ref,
    docs, qbuf, dobuf, kvbuf, bias, ebuf, dpbuf, stat, pbuf, dsbuf, sbuf, ubuf, xbuf, tbuf, rbuf, dqbuf,
    docsem, lsem, qsend, qrecv, kvsend, kvrecv, fsend, frecv, usend, urecv, xsend, xrecv, gsend, grecv, dqsend, dqrecv, dqloc,
):
    me = lax.axis_index("ctx")
    sec = lax.axis_index("section")
    rows = kv_ref.shape[1]
    layers = q_ref.shape[0] // rows
    width = group * layers * rows
    core = lax.rem(me, 2)
    other = 1 - core
    chip = me // 2
    chips = n // 2
    depth = reach // 2
    place = lax.rem(chip, depth)
    blocks = reach + 2
    heads = heads_kv // 2
    gw = group * HD
    window = (reach + 1) * rows
    piece = rows // sections
    scale = HD ** (-0.5)
    paired = sections % 2 == 0
    half = lax.rem(sec, 2)
    mate = sec + 1 - 2 * half

    def dev(ctx, section):
        return {"ctx": ctx, "section": section}

    def cols(head, width):
        return pl.ds(pl.multiple_of(head * width, HD), width)

    def local_copies(h):
        g = core * heads + h
        return [
            pltpu.make_async_copy(q_ref.at[:, cols(g, gw)], qbuf.at[h, core], lsem.at[h, 0]),
            pltpu.make_async_copy(do_ref.at[:, cols(g, gw)], dobuf.at[h, core], lsem.at[h, 1]),
            pltpu.make_async_copy(
                kv_ref.at[:, :, cols(g, HD)], kvbuf.at[h, :, reach + core], lsem.at[h, 2]
            ),
        ]

    def q_copies(h):
        g = other * heads + h
        partner = dev(2 * chip + other, sec)
        return [
            pltpu.make_async_remote_copy(
                src_ref=src.at[:, cols(g, gw)], dst_ref=dst.at[h, core],
                send_sem=qsend.at[h, k], recv_sem=qrecv.at[h, k],
                device_id=partner, device_id_type=MESH,
            )
            for k, (src, dst) in enumerate([(q_ref, qbuf), (do_ref, dobuf)])
        ]

    def kv_copy(h, d, w):
        to = lax.rem(core + w, 2)
        slot = core - 2 * d + reach
        return pltpu.make_async_remote_copy(
            src_ref=kv_ref.at[:, :, cols(to * heads + h, HD)], dst_ref=kvbuf.at[h, :, slot],
            send_sem=kvsend.at[h, d, w], recv_sem=kvrecv.at[h, slot],
            device_id=dev(2 * (chip + d) + to, sec), device_id_type=MESH,
        )

    def kv_half(h, w):
        to = lax.rem(core + w, 2)
        return pltpu.make_async_remote_copy(
            src_ref=kv_ref.at[half, :, cols(to * heads + h, HD)], dst_ref=kvbuf.at[h, half, core],
            send_sem=kvsend.at[h, depth, w], recv_sem=kvrecv.at[h, core],
            device_id=dev(2 * (chip + depth) + to, sec), device_id_type=MESH,
        )

    def kv_wait(h, slot):
        return pltpu.make_async_remote_copy(
            src_ref=kv_ref.at[:, :, pl.ds(0, HD)], dst_ref=kvbuf.at[h, :, slot],
            send_sem=kvsend.at[h, 0, 0], recv_sem=kvrecv.at[h, slot],
            device_id=dev(2 * chip + other, sec), device_id_type=MESH,
        )

    def half_wait(h, slot):
        return pltpu.make_async_remote_copy(
            src_ref=kv_ref.at[half, :, pl.ds(0, HD)], dst_ref=kvbuf.at[h, half, slot],
            send_sem=kvsend.at[h, 0, 0], recv_sem=kvrecv.at[h, slot],
            device_id=dev(2 * chip + other, sec), device_id_type=MESH,
        )

    def forward_copy(h, part):
        return pltpu.make_async_remote_copy(
            src_ref=kvbuf.at[h, part, pl.ds(0, 2)], dst_ref=kvbuf.at[h, part, pl.ds(0, 2)],
            send_sem=fsend.at[h], recv_sem=frecv.at[h],
            device_id=dev(me, mate), device_id_type=MESH,
        )

    def far_sends(h, act):
        @pl.when(chip + depth < chips)
        def _():
            if paired:
                @pl.when(place >= 1)
                def _():
                    for w in range(2):
                        act(kv_half(h, w))

                @pl.when(place < 1)
                def _():
                    for w in range(2):
                        act(kv_copy(h, depth, w))
            else:
                for w in range(2):
                    act(kv_copy(h, depth, w))

    def near_sends(h, act):
        for d in range(depth - 1, 0, -1):
            @pl.when(chip + d < chips)
            def _():
                for w in range(2):
                    act(kv_copy(h, d, w))

    def start(copy):
        copy.start()

    def wait_send(copy):
        copy.wait_send()

    def forward(h):
        if paired:
            @pl.when((place >= 1) & (chip >= depth))
            def _():
                for slot in range(2):
                    half_wait(h, slot).wait_recv()
                forward_copy(h, half).start()

    def kv_arrival(h, pair):
        if pair > 0:
            @pl.when(chip >= depth - pair)
            def _():
                for slot in (2 * pair, 2 * pair + 1):
                    kv_wait(h, slot).wait_recv()

            return

        @pl.when(chip >= depth)
        def _():
            if paired:
                @pl.when(place >= 1)
                def _():
                    forward_copy(h, 1 - half).wait_recv()

                @pl.when(place < 1)
                def _():
                    for slot in range(2):
                        kv_wait(h, slot).wait_recv()
            else:
                for slot in range(2):
                    kv_wait(h, slot).wait_recv()

    def x_copy(h, pair, t, k):
        to = lax.rem(sec + t, sections)
        return pltpu.make_async_remote_copy(
            src_ref=sbuf.at[h, k, pl.ds(2 * pair, 2), pl.ds(pl.multiple_of(to * piece, piece), piece)],
            dst_ref=xbuf.at[h, t - 1, k, pl.ds(2 * pair, 2)],
            send_sem=xsend.at[h, pair, t - 1, k], recv_sem=xrecv.at[h, pair, t - 1, k],
            device_id=dev(me, to), device_id_type=MESH,
        )

    def u_copy(h):
        return pltpu.make_async_remote_copy(
            src_ref=sbuf.at[h, 1, pl.ds(reach - 2, 2)], dst_ref=ubuf.at[h],
            send_sem=usend.at[h], recv_sem=urecv.at[h],
            device_id=dev(2 * (chip - 1) + core, sec), device_id_type=MESH,
        )

    def g_copy(h, k, slot):
        d = (reach + 1 - slot) // 2
        return pltpu.make_async_remote_copy(
            src_ref=tbuf.at[h, slot, k], dst_ref=rbuf.at[d, core, h, k],
            send_sem=gsend.at[h, slot, k], recv_sem=grecv.at[d, core, h, k],
            device_id=dev(2 * (chip - d) + (slot - reach) % 2, sec), device_id_type=MESH,
        )

    def g_wait(h, k, d, c):
        return pltpu.make_async_remote_copy(
            src_ref=tbuf.at[h, 0, k], dst_ref=rbuf.at[d, c, h, k],
            send_sem=gsend.at[h, 0, k], recv_sem=grecv.at[d, c, h, k],
            device_id=dev(2 * chip + other, sec), device_id_type=MESH,
        )

    def when_pair(pair, run):
        if pair < depth:
            pl.when(chip >= depth - pair)(run)
        else:
            run()

    def when_sent(slot, run):
        if slot < reach:
            run()
        else:
            pl.when(core != slot - reach)(run)

    def scatter(h, k, pairs):
        def send(pair):
            for t in range(1, sections):
                x_copy(h, pair, t, k).start()

        for pair in pairs:
            when_pair(pair, functools.partial(send, pair))

    def deliver(h, k, pairs):
        own = pl.ds(pl.multiple_of(sec * piece, piece), piece)

        def run(pair):
            for t in range(1, sections):
                x_copy(h, pair, t, k).wait_recv()
            for slot in (2 * pair, 2 * pair + 1):
                total = sbuf[h, k, slot, own].astype(jnp.float32)
                for t in range(1, sections):
                    total = total + xbuf[h, t - 1, k, slot].astype(jnp.float32)
                tbuf[h, slot, k] = total.astype(jnp.bfloat16)
                when_sent(slot, lambda: g_copy(h, k, slot).start())

        for pair in pairs:
            when_pair(pair, functools.partial(run, pair))

    def dq_copy(h):
        return pltpu.make_async_remote_copy(
            src_ref=dqbuf.at[h, other], dst_ref=dq_ref.at[:, cols(core * heads + h, gw)],
            send_sem=dqsend.at[h], recv_sem=dqrecv.at[h],
            device_id=dev(2 * chip + other, sec), device_id_type=MESH,
        )

    def dq_wait(h):
        return pltpu.make_async_remote_copy(
            src_ref=dqbuf.at[h, other], dst_ref=dq_ref.at[:, cols(other * heads + h, gw)],
            send_sem=dqsend.at[h], recv_sem=dqrecv.at[h],
            device_id=dev(2 * chip + other, sec), device_id_type=MESH,
        )

    def dq_local(h):
        return pltpu.make_async_copy(
            dqbuf.at[h, core], dq_ref.at[:, cols(core * heads + h, gw)], dqloc.at[h]
        )

    barrier = pltpu.get_barrier_semaphore()

    def greet(ctx, section):
        pl.semaphore_signal(barrier, inc=1, device_id=dev(ctx, section), device_id_type=MESH)

    for t in range(1, sections):
        greet(me, lax.rem(sec + t, sections))
    for step in range(-depth, depth + 1):
        @pl.when((chip + step >= 0) & (chip + step < chips))
        def _():
            for w in range(2):
                if step == 0 and w == 0:
                    continue
                greet(2 * (chip + step) + lax.rem(core + w, 2), sec)

    docs_copy = pltpu.make_async_copy(docs_ref, docs, docsem)
    docs_copy.start()
    for h in range(heads):
        for copy in local_copies(h):
            copy.start()

    near = jnp.minimum(chip, depth) + jnp.minimum(chips - 1 - chip, depth)
    pl.semaphore_wait(barrier, 2 * near + 1 + sections - 1)

    far_sends(0, start)
    near_sends(0, start)
    for h in range(heads):
        for copy in q_copies(h):
            copy.start()
        kv_copy(h, 0, 1).start()

    for d in range(1, depth + 1):
        @pl.when(chip - d < 0)
        def _():
            for slot in (reach - 2 * d, reach - 2 * d + 1):
                for h in range(heads):
                    kvbuf[h, :, slot] = jnp.zeros((2, rows, HD), jnp.bfloat16)

        @pl.when(chip + d >= chips)
        def _():
            rbuf[d] = jnp.zeros(rbuf.shape[1:], jnp.bfloat16)

    for h in range(heads):
        dsbuf[h, 0:rows, width : 2 * width] = jnp.zeros((rows, width), jnp.bfloat16)
        dsbuf[h, (reach + 1) * rows : blocks * rows, 0:width] = jnp.zeros((rows, width), jnp.bfloat16)
    docs_copy.wait()
    row_at = lax.broadcasted_iota(jnp.int32, (rows, rows), 0)
    col_at = lax.broadcasted_iota(jnp.int32, (rows, rows), 1)
    for slot in range(blocks):
        at = 2 * chip - reach + slot
        kdoc = docs[pl.ds(jnp.maximum(at, 0), 1), :].astype(jnp.float32)
        kdoc = jnp.transpose(jnp.broadcast_to(kdoc, (rows, rows)))
        for sub in range(2):
            if not 0 <= slot - sub <= reach:
                continue
            qdoc = docs[pl.ds(2 * chip + sub, 1), :].astype(jnp.float32)
            kplace = at * rows + row_at
            qplace = (2 * chip + sub) * rows + col_at
            seen = (kplace <= qplace) & (kplace >= 0) & (kdoc == qdoc)
            bias[sub, (slot - sub) * rows : (slot - sub + 1) * rows] = jnp.where(seen, 0.0, NEG)

    def stacked(h, k, sub):
        buf = (qbuf, dobuf)[k]
        return jnp.concatenate([buf[h, sub, :, i * HD : (i + 1) * HD] for i in range(group)], axis=0)

    def part_rows(sub, part):
        if part == 0:
            return slice((reach - sub) * rows, window)
        return slice(max(2 * part - 2 - sub, 0) * rows, (2 * part - sub) * rows)

    def score_part(h, sub, part):
        at = part_rows(sub, part)
        slots = slice(at.start // rows + sub, at.stop // rows + sub)
        k = kvbuf[h, 0, slots].reshape(at.stop - at.start, HD)
        v = kvbuf[h, 1, slots].reshape(at.stop - at.start, HD)
        nt = (((1,), (1,)), ((), ()))
        s = lax.dot_general(k, stacked(h, 0, sub), nt, preferred_element_type=jnp.float32)
        dp = lax.dot_general(v, stacked(h, 1, sub), nt, preferred_element_type=jnp.float32)
        s = s * (scale * LOG2E) + jnp.concatenate([bias[sub, at]] * (layers * group), axis=1)
        top = jnp.max(s, axis=0, keepdims=True)
        e = jnp.exp2(s - top)
        ebuf[h, sub, at] = e
        dpbuf[h, sub, at] = dp
        stat[h, sub, part, 0:1] = top
        stat[h, sub, part, 1:2] = jnp.sum(e, axis=0, keepdims=True)
        stat[h, sub, part, 2:3] = jnp.sum(e * dp, axis=0, keepdims=True)

    def prob_part(h, k, sub):
        parts = range(depth + 1)
        tops = [stat[h, sub, part, 0:1] for part in parts]
        top = functools.reduce(jnp.maximum, tops)
        factors = [jnp.exp2(t - top) for t in tops]
        inverse = 1.0 / sum(factors[part] * stat[h, sub, part, 1:2] for part in parts)
        factors = [f * inverse for f in factors]
        delta = sum(factors[part] * stat[h, sub, part, 2:3] for part in parts)
        for part in parts:
            at = part_rows(sub, part)
            keys_at = slice(at.start + sub * rows, at.stop + sub * rows)
            for i in range(group):
                span = slice(i * layers * rows, (i + 1) * layers * rows)
                p = ebuf[h, sub, at, span] * factors[part][:, span]
                to = slice(sub * width + span.start, sub * width + span.stop)
                if k == 1:
                    pbuf[keys_at, to] = p.astype(jnp.bfloat16)
                else:
                    ds = p * (dpbuf[h, sub, at, span] - delta[:, span])
                    dsbuf[h, keys_at, to] = ds.astype(jnp.bfloat16)

    def key_part(h, k):
        stack = jnp.concatenate([stacked(h, k, sub) for sub in range(2)], axis=0)
        at = slice(rows, (reach + 1) * rows)
        total = jnp.dot(dsbuf[h, at] if k == 0 else pbuf[at], stack, preferred_element_type=jnp.float32)
        total = total * scale if k == 0 else total
        sbuf[h, k, 1 : reach + 1] = total.astype(jnp.bfloat16).reshape(reach, rows, HD)

    def edge_part(h, k, slot, sub):
        at = slice(slot * rows, (slot + 1) * rows)
        to = slice(sub * width, (sub + 1) * width)
        weights = dsbuf[h, at, to] if k == 0 else pbuf[at, to]
        total = jnp.dot(weights, stacked(h, k, sub), preferred_element_type=jnp.float32)
        sbuf[h, k, slot] = (total * scale if k == 0 else total).astype(jnp.bfloat16)

    def query_part(h, sub):
        kt = jnp.transpose(kvbuf[h, 0].reshape(blocks * rows, HD))
        to = pl.ds(pl.multiple_of(sub * width, rows), width)
        dqt = jnp.dot(kt, dsbuf[h, :, to], preferred_element_type=jnp.float32) * scale
        for i in range(group):
            dqbuf[h, sub, :, i * HD : (i + 1) * HD] = jnp.transpose(
                dqt[:, i * layers * rows : (i + 1) * layers * rows]
            ).astype(jnp.bfloat16)

    def own_scores(h, unused):
        for copy in local_copies(h):
            copy.wait()
        for copy in q_copies(h):
            copy.wait_recv()
        for c in range(2):
            pl.when(core != c)(lambda: kv_wait(h, reach + c).wait_recv())
        for sub in range(2):
            score_part(h, sub, 0)
        return unused

    own_scores(0, 0)
    forward(0)
    for h in range(1, heads):
        far_sends(h - 1, wait_send)
        far_sends(h, start)
        near_sends(h - 1, wait_send)
        near_sends(h, start)
        own_scores(h, 0)

    last = heads - 1
    far, near = range(depth), range(depth, depth + 1)

    def head_step(h, unused):
        def scores(order):
            for pair in order:
                kv_arrival(h, pair)
                if pair == 0:
                    pl.when(h + 1 < heads)(lambda: forward(h + 1))
                for sub in range(2):
                    score_part(h, sub, pair + 1)

        pl.when(place < 1)(lambda: scores(range(depth)))
        pl.when(place >= 1)(lambda: scores(range(depth - 1, -1, -1)))
        for k in (1, 0):
            pl.when(h > 0)(lambda: deliver(h - 1, k, range(depth - k)))
            for sub in range(2):
                prob_part(h, k, sub)
            key_part(h, k)
            edge_part(h, k, 0, 0)
            scatter(h, k, range(depth - 1))
            if k == 1:
                pl.when(h == last)(lambda: scatter(h, k, range(depth - 1, depth)))
                pl.when((h < last) & (chip >= 1))(lambda: u_copy(h).start())
            else:
                scatter(h, k, range(depth - 1, depth))
        for k in (0, 1):
            edge_part(h, k, reach + 1, 1)
            if k == 0:
                pl.when(h < last)(lambda: scatter(h, k, near))
        return unused

    lax.fori_loop(0, heads, head_step, 0)
    for h in range(heads):
        if h < last:
            @pl.when(chip + 1 < chips)
            def _():
                u_copy(h).wait_recv()
                own = sbuf[h, 1, reach:blocks].astype(jnp.float32) + ubuf[h].astype(jnp.float32)
                sbuf[h, 1, reach:blocks] = own.astype(jnp.bfloat16)

        scatter(h, 1, near)
    scatter(last, 0, near)

    def queries(h):
        query_part(h, other)
        dq_copy(h).start()
        query_part(h, core)
        dq_local(h).start()

    for h in range(last):
        queries(h)
    deliver(last, 1, far)
    query_part(last, other)
    dq_copy(last).start()
    deliver(last, 0, far)
    query_part(last, core)
    dq_local(last).start()

    def own_step(h, unused):
        for k in (1, 0):
            deliver(h, k, near)
            rbuf[0, core, h, k] = tbuf[h, reach + core, k]
        return unused

    lax.fori_loop(0, heads, own_step, 0)

    def collect(h, k):
        steps = [d for d in range(depth, 0, -1) if d > 1 or h == last or k == 0]
        for c in range(2):
            for d in steps + [0]:
                pl.when(core != c if d == 0 else chip + d < chips)(lambda: g_wait(h, k, d, c).wait_recv())
            total = rbuf[0, c, h, k].astype(jnp.float32)
            for d in steps:
                total = total + rbuf[d, c, h, k].astype(jnp.float32)
            g = c * heads + h
            out_ref[k, :, g * HD : (g + 1) * HD] = total.astype(jnp.bfloat16)

    for h in range(heads):
        for k in (1, 0):
            if h < last or k == 1:
                collect(h, k)

    def finish(h):
        dq_wait(h).wait_recv()
        dq_copy(h).wait_send()
        dq_local(h).wait()
        for copy in q_copies(h):
            copy.wait_send()
        kv_copy(h, 0, 1).wait_send()
        if h == last:
            far_sends(h, wait_send)
            near_sends(h, wait_send)
        if paired:
            @pl.when((place >= 1) & (chip >= depth))
            def _():
                forward_copy(h, half).wait_send()

        def sent(pair, k):
            for t in range(1, sections):
                x_copy(h, pair, t, k).wait_send()
            for slot in (2 * pair, 2 * pair + 1):
                when_sent(slot, lambda: g_copy(h, k, slot).wait_send())

        for pair in range(depth + 1):
            for k in range(2):
                if pair == depth - 1 and h < last and k == 1:
                    pl.when(chip >= 1)(lambda: u_copy(h).wait_send())
                else:
                    when_pair(pair, functools.partial(sent, pair, k))

    for h in range(heads):
        finish(h)
    collect(last, 0)


def body(queries, grad_out, keys_values, doc_ids):
    layers, rows, width = queries.shape
    kv_width = keys_values.shape[2]
    heads_kv = kv_width // HD
    group = width // kv_width
    n = lax.axis_size("ctx")
    sections = lax.axis_size("section")
    reach = n // 4
    heads = heads_kv // 2
    blocks = reach + 2
    window = (reach + 1) * rows
    piece = rows // sections
    depth = reach // 2
    bf, f32 = jnp.bfloat16, jnp.float32
    dma = pltpu.SemaphoreType.DMA
    hbm = pl.BlockSpec(memory_space=pl.ANY)
    vmem = pl.BlockSpec(memory_space=pltpu.VMEM)
    grad_queries, grad_kv = pl.pallas_call(
        functools.partial(kernel, n, sections, reach, heads_kv, group),
        out_shape=(
            jax.ShapeDtypeStruct((layers * rows, width), bf),
            jax.ShapeDtypeStruct((2, piece, kv_width), bf),
        ),
        in_specs=[hbm, hbm, hbm, hbm],
        out_specs=(hbm, vmem),
        scratch_shapes=[
            pltpu.VMEM((n, rows), jnp.int32),
            pltpu.VMEM((heads, 2, layers * rows, group * HD), bf),
            pltpu.VMEM((heads, 2, layers * rows, group * HD), bf),
            pltpu.VMEM((heads, 2, blocks, rows, HD), bf),
            pltpu.VMEM((2, window, rows), f32),
            pltpu.VMEM((heads, 2, window, group * layers * rows), f32),
            pltpu.VMEM((heads, 2, window, group * layers * rows), f32),
            pltpu.VMEM((heads, 2, depth + 1, 8, group * layers * rows), f32),
            pltpu.VMEM((blocks * rows, 2 * group * layers * rows), bf),
            pltpu.VMEM((heads, blocks * rows, 2 * group * layers * rows), bf),
            pltpu.VMEM((heads, 2, blocks, rows, HD), bf),
            pltpu.VMEM((heads, 2, rows, HD), bf),
            pltpu.VMEM((heads, max(sections - 1, 1), 2, blocks, piece, HD), bf),
            pltpu.VMEM((heads, blocks, 2, piece, HD), bf),
            pltpu.VMEM((depth + 1, 2, heads, 2, piece, HD), bf),
            pltpu.VMEM((heads, 2, layers * rows, group * HD), bf),
            dma,
            dma((heads, 3)),
            dma((heads, 2)),
            dma((heads, 2)),
            dma((heads, depth + 1, 2)),
            dma((heads, blocks)),
            dma((heads,)),
            dma((heads,)),
            dma((heads,)),
            dma((heads,)),
            dma((heads, depth + 1, max(sections - 1, 1), 2)),
            dma((heads, depth + 1, max(sections - 1, 1), 2)),
            dma((heads, blocks, 2)),
            dma((depth + 1, 2, heads, 2)),
            dma((heads,)),
            dma((heads,)),
            dma((heads,)),
        ],
        compiler_params=pltpu.CompilerParams(
            collective_id=0, has_side_effects=True, vmem_limit_bytes=(24 + 4 * reach) * 1024 * 1024
        ),
        name="cross_backward",
    )(
        *[
            pltpu.with_memory_space_constraint(x, pltpu.HBM)
            for x in (
                queries.reshape(layers * rows, width), grad_out.reshape(layers * rows, width),
                keys_values, doc_ids.reshape(n, rows),
            )
        ]
    )
    return grad_queries.reshape(queries.shape), grad_kv


def solution(mesh):
    return jax.shard_map(
        body,
        mesh=mesh,
        in_specs=(P("section", "ctx", None), P("section", "ctx", None), P(None, "ctx", None), P()),
        out_specs=(P("section", "ctx", None), P(None, ("ctx", "section"), None)),
        check_vma=False,
    )
```

```python
import functools

import jax
import jax.numpy as jnp
from jax import lax
from jax.experimental import pallas as pl
from jax.experimental.pallas import tpu as pltpu
from jax.sharding import PartitionSpec as P

HD = 128
MESH = pl.DeviceIdType.MESH
LOG2E = 1.4426950408889634
NEG = -1e30


def kernel(
    n, sections, reach, heads_kv, group,
    q_ref, do_ref, kv_ref, docs_ref,
    dq_ref, out_ref,
    docs, qbuf, dobuf, kvbuf, bias, ebuf, dpbuf, stat, pbuf, dsbuf, sbuf, ubuf, xbuf, tbuf, rbuf, dqbuf,
    docsem, lsem, qsend, qrecv, kvsend, kvrecv, fsend, frecv, usend, urecv, xsend, xrecv, gsend, grecv, dqsend, dqrecv, dqloc,
):
    me = lax.axis_index("ctx")
    sec = lax.axis_index("section")
    rows = kv_ref.shape[1]
    layers = q_ref.shape[0] // rows
    width = group * layers * rows
    core = lax.rem(me, 2)
    other = 1 - core
    chip = me // 2
    chips = n // 2
    depth = reach // 2
    place = lax.rem(chip, depth)
    blocks = reach + 2
    heads = heads_kv // 2
    gw = group * HD
    window = (reach + 1) * rows
    piece = rows // sections
    scale = HD ** (-0.5)
    paired = sections % 2 == 0
    half = lax.rem(sec, 2)
    mate = sec + 1 - 2 * half

    def dev(ctx, section):
        return {"ctx": ctx, "section": section}

    def cols(head, width):
        return pl.ds(pl.multiple_of(head * width, HD), width)

    def local_copies(h):
        g = core * heads + h
        return [
            pltpu.make_async_copy(q_ref.at[:, cols(g, gw)], qbuf.at[h, core], lsem.at[h, 0]),
            pltpu.make_async_copy(do_ref.at[:, cols(g, gw)], dobuf.at[h, core], lsem.at[h, 1]),
            pltpu.make_async_copy(
                kv_ref.at[:, :, cols(g, HD)], kvbuf.at[h, :, reach + core], lsem.at[h, 2]
            ),
        ]

    def q_copies(h):
        g = other * heads + h
        partner = dev(2 * chip + other, sec)
        return [
            pltpu.make_async_remote_copy(
                src_ref=src.at[:, cols(g, gw)], dst_ref=dst.at[h, core],
                send_sem=qsend.at[h, k], recv_sem=qrecv.at[h, k],
                device_id=partner, device_id_type=MESH,
            )
            for k, (src, dst) in enumerate([(q_ref, qbuf), (do_ref, dobuf)])
        ]

    def kv_copy(h, d, w):
        to = lax.rem(core + w, 2)
        slot = core - 2 * d + reach
        return pltpu.make_async_remote_copy(
            src_ref=kv_ref.at[:, :, cols(to * heads + h, HD)], dst_ref=kvbuf.at[h, :, slot],
            send_sem=kvsend.at[h, d, w], recv_sem=kvrecv.at[h, slot],
            device_id=dev(2 * (chip + d) + to, sec), device_id_type=MESH,
        )

    def kv_half(h, w):
        to = lax.rem(core + w, 2)
        return pltpu.make_async_remote_copy(
            src_ref=kv_ref.at[half, :, cols(to * heads + h, HD)], dst_ref=kvbuf.at[h, half, core],
            send_sem=kvsend.at[h, depth, w], recv_sem=kvrecv.at[h, core],
            device_id=dev(2 * (chip + depth) + to, sec), device_id_type=MESH,
        )

    def kv_wait(h, slot):
        return pltpu.make_async_remote_copy(
            src_ref=kv_ref.at[:, :, pl.ds(0, HD)], dst_ref=kvbuf.at[h, :, slot],
            send_sem=kvsend.at[h, 0, 0], recv_sem=kvrecv.at[h, slot],
            device_id=dev(2 * chip + other, sec), device_id_type=MESH,
        )

    def half_wait(h, slot):
        return pltpu.make_async_remote_copy(
            src_ref=kv_ref.at[half, :, pl.ds(0, HD)], dst_ref=kvbuf.at[h, half, slot],
            send_sem=kvsend.at[h, 0, 0], recv_sem=kvrecv.at[h, slot],
            device_id=dev(2 * chip + other, sec), device_id_type=MESH,
        )

    def forward_copy(h, part):
        return pltpu.make_async_remote_copy(
            src_ref=kvbuf.at[h, part, pl.ds(0, 2)], dst_ref=kvbuf.at[h, part, pl.ds(0, 2)],
            send_sem=fsend.at[h], recv_sem=frecv.at[h],
            device_id=dev(me, mate), device_id_type=MESH,
        )

    def far_sends(h, act):
        @pl.when(chip + depth < chips)
        def _():
            if paired:
                @pl.when(place >= 1)
                def _():
                    for w in range(2):
                        act(kv_half(h, w))

                @pl.when(place < 1)
                def _():
                    for w in range(2):
                        act(kv_copy(h, depth, w))
            else:
                for w in range(2):
                    act(kv_copy(h, depth, w))

    def near_sends(h, act):
        for d in range(depth - 1, 0, -1):
            @pl.when(chip + d < chips)
            def _():
                for w in range(2):
                    act(kv_copy(h, d, w))

    def start(copy):
        copy.start()

    def wait_send(copy):
        copy.wait_send()

    def forward(h):
        if paired:
            @pl.when((place >= 1) & (chip >= depth))
            def _():
                for slot in range(2):
                    half_wait(h, slot).wait_recv()
                forward_copy(h, half).start()

    def kv_arrival(h, pair):
        if pair > 0:
            @pl.when(chip >= depth - pair)
            def _():
                for slot in (2 * pair, 2 * pair + 1):
                    kv_wait(h, slot).wait_recv()

            return

        @pl.when(chip >= depth)
        def _():
            if paired:
                @pl.when(place >= 1)
                def _():
                    forward_copy(h, 1 - half).wait_recv()

                @pl.when(place < 1)
                def _():
                    for slot in range(2):
                        kv_wait(h, slot).wait_recv()
            else:
                for slot in range(2):
                    kv_wait(h, slot).wait_recv()

    def x_copy(h, pair, t, k):
        to = lax.rem(sec + t, sections)
        return pltpu.make_async_remote_copy(
            src_ref=sbuf.at[h, k, pl.ds(2 * pair, 2), pl.ds(pl.multiple_of(to * piece, piece), piece)],
            dst_ref=xbuf.at[h, t - 1, k, pl.ds(2 * pair, 2)],
            send_sem=xsend.at[h, pair, t - 1, k], recv_sem=xrecv.at[h, pair, t - 1, k],
            device_id=dev(me, to), device_id_type=MESH,
        )

    def u_copy(h):
        return pltpu.make_async_remote_copy(
            src_ref=sbuf.at[h, 1, pl.ds(reach - 2, 2)], dst_ref=ubuf.at[h],
            send_sem=usend.at[h], recv_sem=urecv.at[h],
            device_id=dev(2 * (chip - 1) + core, sec), device_id_type=MESH,
        )

    def g_copy(h, k, slot):
        d = (reach + 1 - slot) // 2
        return pltpu.make_async_remote_copy(
            src_ref=tbuf.at[h, slot, k], dst_ref=rbuf.at[d, core, h, k],
            send_sem=gsend.at[h, slot, k], recv_sem=grecv.at[d, core, h, k],
            device_id=dev(2 * (chip - d) + (slot - reach) % 2, sec), device_id_type=MESH,
        )

    def g_wait(h, k, d, c):
        return pltpu.make_async_remote_copy(
            src_ref=tbuf.at[h, 0, k], dst_ref=rbuf.at[d, c, h, k],
            send_sem=gsend.at[h, 0, k], recv_sem=grecv.at[d, c, h, k],
            device_id=dev(2 * chip + other, sec), device_id_type=MESH,
        )

    def when_pair(pair, run):
        if pair < depth:
            pl.when(chip >= depth - pair)(run)
        else:
            run()

    def when_sent(slot, run):
        if slot < reach:
            run()
        else:
            pl.when(core != slot - reach)(run)

    def scatter(h, k, pairs):
        def send(pair):
            for t in range(1, sections):
                x_copy(h, pair, t, k).start()

        for pair in pairs:
            when_pair(pair, functools.partial(send, pair))

    def deliver(h, k, pairs):
        own = pl.ds(pl.multiple_of(sec * piece, piece), piece)

        def run(pair):
            for t in range(1, sections):
                x_copy(h, pair, t, k).wait_recv()
            for slot in (2 * pair, 2 * pair + 1):
                total = sbuf[h, k, slot, own].astype(jnp.float32)
                for t in range(1, sections):
                    total = total + xbuf[h, t - 1, k, slot].astype(jnp.float32)
                tbuf[h, slot, k] = total.astype(jnp.bfloat16)
                when_sent(slot, lambda: g_copy(h, k, slot).start())

        for pair in pairs:
            when_pair(pair, functools.partial(run, pair))

    def dq_copy(h):
        return pltpu.make_async_remote_copy(
            src_ref=dqbuf.at[h, other], dst_ref=dq_ref.at[:, cols(core * heads + h, gw)],
            send_sem=dqsend.at[h], recv_sem=dqrecv.at[h],
            device_id=dev(2 * chip + other, sec), device_id_type=MESH,
        )

    def dq_wait(h):
        return pltpu.make_async_remote_copy(
            src_ref=dqbuf.at[h, other], dst_ref=dq_ref.at[:, cols(other * heads + h, gw)],
            send_sem=dqsend.at[h], recv_sem=dqrecv.at[h],
            device_id=dev(2 * chip + other, sec), device_id_type=MESH,
        )

    def dq_local(h):
        return pltpu.make_async_copy(
            dqbuf.at[h, core], dq_ref.at[:, cols(core * heads + h, gw)], dqloc.at[h]
        )

    barrier = pltpu.get_barrier_semaphore()

    def greet(ctx, section):
        pl.semaphore_signal(barrier, inc=1, device_id=dev(ctx, section), device_id_type=MESH)

    for t in range(1, sections):
        greet(me, lax.rem(sec + t, sections))
    for step in range(-depth, depth + 1):
        @pl.when((chip + step >= 0) & (chip + step < chips))
        def _():
            for w in range(2):
                if step == 0 and w == 0:
                    continue
                greet(2 * (chip + step) + lax.rem(core + w, 2), sec)

    docs_copy = pltpu.make_async_copy(docs_ref, docs, docsem)
    docs_copy.start()
    for h in range(heads):
        for copy in local_copies(h):
            copy.start()

    near = jnp.minimum(chip, depth) + jnp.minimum(chips - 1 - chip, depth)
    pl.semaphore_wait(barrier, 2 * near + 1 + sections - 1)

    far_sends(0, start)
    near_sends(0, start)
    for h in range(heads):
        for copy in q_copies(h):
            copy.start()
        kv_copy(h, 0, 1).start()

    for d in range(1, depth + 1):
        @pl.when(chip - d < 0)
        def _():
            for slot in (reach - 2 * d, reach - 2 * d + 1):
                for h in range(heads):
                    kvbuf[h, :, slot] = jnp.zeros((2, rows, HD), jnp.bfloat16)

        @pl.when(chip + d >= chips)
        def _():
            rbuf[d] = jnp.zeros(rbuf.shape[1:], jnp.bfloat16)

    for h in range(heads):
        dsbuf[h, 0:rows, width : 2 * width] = jnp.zeros((rows, width), jnp.bfloat16)
        dsbuf[h, (reach + 1) * rows : blocks * rows, 0:width] = jnp.zeros((rows, width), jnp.bfloat16)
    docs_copy.wait()
    row_at = lax.broadcasted_iota(jnp.int32, (rows, rows), 0)
    col_at = lax.broadcasted_iota(jnp.int32, (rows, rows), 1)
    for slot in range(blocks):
        at = 2 * chip - reach + slot
        kdoc = docs[pl.ds(jnp.maximum(at, 0), 1), :].astype(jnp.float32)
        kdoc = jnp.transpose(jnp.broadcast_to(kdoc, (rows, rows)))
        for sub in range(2):
            if not 0 <= slot - sub <= reach:
                continue
            qdoc = docs[pl.ds(2 * chip + sub, 1), :].astype(jnp.float32)
            kplace = at * rows + row_at
            qplace = (2 * chip + sub) * rows + col_at
            seen = (kplace <= qplace) & (kplace >= 0) & (kdoc == qdoc)
            bias[sub, (slot - sub) * rows : (slot - sub + 1) * rows] = jnp.where(seen, 0.0, NEG)

    def stacked(h, k, sub):
        buf = (qbuf, dobuf)[k]
        return jnp.concatenate([buf[h, sub, :, i * HD : (i + 1) * HD] for i in range(group)], axis=0)

    def part_rows(sub, part):
        if part == 0:
            return slice((reach - sub) * rows, window)
        return slice(max(2 * part - 2 - sub, 0) * rows, (2 * part - sub) * rows)

    def score_part(h, sub, part):
        at = part_rows(sub, part)
        slots = slice(at.start // rows + sub, at.stop // rows + sub)
        k = kvbuf[h, 0, slots].reshape(at.stop - at.start, HD)
        v = kvbuf[h, 1, slots].reshape(at.stop - at.start, HD)
        nt = (((1,), (1,)), ((), ()))
        s = lax.dot_general(k, stacked(h, 0, sub), nt, preferred_element_type=jnp.float32)
        dp = lax.dot_general(v, stacked(h, 1, sub), nt, preferred_element_type=jnp.float32)
        s = s * (scale * LOG2E) + jnp.concatenate([bias[sub, at]] * (layers * group), axis=1)
        top = jnp.max(s, axis=0, keepdims=True)
        e = jnp.exp2(s - top)
        ebuf[h, sub, at] = e
        dpbuf[h, sub, at] = dp
        stat[h, sub, part, 0:1] = top
        stat[h, sub, part, 1:2] = jnp.sum(e, axis=0, keepdims=True)
        stat[h, sub, part, 2:3] = jnp.sum(e * dp, axis=0, keepdims=True)

    def prob_part(h, k, sub):
        parts = range(depth + 1)
        tops = [stat[h, sub, part, 0:1] for part in parts]
        top = functools.reduce(jnp.maximum, tops)
        factors = [jnp.exp2(t - top) for t in tops]
        inverse = 1.0 / sum(factors[part] * stat[h, sub, part, 1:2] for part in parts)
        factors = [f * inverse for f in factors]
        delta = sum(factors[part] * stat[h, sub, part, 2:3] for part in parts)
        for part in parts:
            at = part_rows(sub, part)
            keys_at = slice(at.start + sub * rows, at.stop + sub * rows)
            for i in range(group):
                span = slice(i * layers * rows, (i + 1) * layers * rows)
                p = ebuf[h, sub, at, span] * factors[part][:, span]
                to = slice(sub * width + span.start, sub * width + span.stop)
                if k == 1:
                    pbuf[keys_at, to] = p.astype(jnp.bfloat16)
                else:
                    ds = p * (dpbuf[h, sub, at, span] - delta[:, span])
                    dsbuf[h, keys_at, to] = ds.astype(jnp.bfloat16)

    def key_part(h, k):
        stack = jnp.concatenate([stacked(h, k, sub) for sub in range(2)], axis=0)
        at = slice(rows, (reach + 1) * rows)
        total = jnp.dot(dsbuf[h, at] if k == 0 else pbuf[at], stack, preferred_element_type=jnp.float32)
        total = total * scale if k == 0 else total
        sbuf[h, k, 1 : reach + 1] = total.astype(jnp.bfloat16).reshape(reach, rows, HD)

    def edge_part(h, k, slot, sub):
        at = slice(slot * rows, (slot + 1) * rows)
        to = slice(sub * width, (sub + 1) * width)
        weights = dsbuf[h, at, to] if k == 0 else pbuf[at, to]
        total = jnp.dot(weights, stacked(h, k, sub), preferred_element_type=jnp.float32)
        sbuf[h, k, slot] = (total * scale if k == 0 else total).astype(jnp.bfloat16)

    def query_part(h, sub):
        kt = jnp.transpose(kvbuf[h, 0].reshape(blocks * rows, HD))
        to = pl.ds(pl.multiple_of(sub * width, rows), width)
        dqt = jnp.dot(kt, dsbuf[h, :, to], preferred_element_type=jnp.float32) * scale
        for i in range(group):
            dqbuf[h, sub, :, i * HD : (i + 1) * HD] = jnp.transpose(
                dqt[:, i * layers * rows : (i + 1) * layers * rows]
            ).astype(jnp.bfloat16)

    def own_scores(h, unused):
        for copy in local_copies(h):
            copy.wait()
        for copy in q_copies(h):
            copy.wait_recv()
        for c in range(2):
            pl.when(core != c)(lambda: kv_wait(h, reach + c).wait_recv())
        for sub in range(2):
            score_part(h, sub, 0)
        return unused

    own_scores(0, 0)
    forward(0)
    for h in range(1, heads):
        far_sends(h - 1, wait_send)
        far_sends(h, start)
        near_sends(h - 1, wait_send)
        near_sends(h, start)
        own_scores(h, 0)

    last = heads - 1
    far, near = range(depth), range(depth, depth + 1)

    def head_step(h, unused):
        def scores(order):
            for pair in order:
                kv_arrival(h, pair)
                if pair == 0:
                    pl.when(h + 1 < heads)(lambda: forward(h + 1))
                for sub in range(2):
                    score_part(h, sub, pair + 1)

        pl.when(place < 1)(lambda: scores(range(depth)))
        pl.when(place >= 1)(lambda: scores(range(depth - 1, -1, -1)))
        for k in (1, 0):
            pl.when(h > 0)(lambda: deliver(h - 1, k, range(depth - k)))
            for sub in range(2):
                prob_part(h, k, sub)
            key_part(h, k)
            edge_part(h, k, 0, 0)
            scatter(h, k, range(depth - 1))
            if k == 1:
                pl.when(chip >= 1)(lambda: u_copy(h).start())
            else:
                scatter(h, k, range(depth - 1, depth))
        for k in (0, 1):
            edge_part(h, k, reach + 1, 1)
            if k == 0:
                pl.when(h < last)(lambda: scatter(h, k, near))
        return unused

    lax.fori_loop(0, heads, head_step, 0)
    def own_values(h):
        @pl.when(chip + 1 < chips)
        def _():
            u_copy(h).wait_recv()
            own = sbuf[h, 1, reach:blocks].astype(jnp.float32) + ubuf[h].astype(jnp.float32)
            sbuf[h, 1, reach:blocks] = own.astype(jnp.bfloat16)

        scatter(h, 1, near)

    for h in range(last):
        own_values(h)
    scatter(last, 0, near)

    def queries(h):
        query_part(h, other)
        dq_copy(h).start()
        query_part(h, core)
        dq_local(h).start()

    for h in range(last):
        queries(h)
    deliver(last, 1, range(depth - 1))
    query_part(last, other)
    dq_copy(last).start()
    own_values(last)
    deliver(last, 0, far)
    query_part(last, core)
    dq_local(last).start()

    def own_step(h, unused):
        for k in (1, 0):
            deliver(h, k, near)
            rbuf[0, core, h, k] = tbuf[h, reach + core, k]
        return unused

    lax.fori_loop(0, heads, own_step, 0)

    def collect(h, k):
        steps = [d for d in range(depth, 0, -1) if d > 1 or k == 0]
        for c in range(2):
            for d in steps + [0]:
                pl.when(core != c if d == 0 else chip + d < chips)(lambda: g_wait(h, k, d, c).wait_recv())
            total = rbuf[0, c, h, k].astype(jnp.float32)
            for d in steps:
                total = total + rbuf[d, c, h, k].astype(jnp.float32)
            g = c * heads + h
            out_ref[k, :, g * HD : (g + 1) * HD] = total.astype(jnp.bfloat16)

    for h in range(heads):
        for k in (1, 0):
            if h < last or k == 1:
                collect(h, k)

    def finish(h):
        dq_wait(h).wait_recv()
        dq_copy(h).wait_send()
        dq_local(h).wait()
        for copy in q_copies(h):
            copy.wait_send()
        kv_copy(h, 0, 1).wait_send()
        if h == last:
            far_sends(h, wait_send)
            near_sends(h, wait_send)
        if paired:
            @pl.when((place >= 1) & (chip >= depth))
            def _():
                forward_copy(h, half).wait_send()

        def sent(pair, k):
            for t in range(1, sections):
                x_copy(h, pair, t, k).wait_send()
            for slot in (2 * pair, 2 * pair + 1):
                when_sent(slot, lambda: g_copy(h, k, slot).wait_send())

        for pair in range(depth + 1):
            for k in range(2):
                if pair == depth - 1 and k == 1:
                    pl.when(chip >= 1)(lambda: u_copy(h).wait_send())
                else:
                    when_pair(pair, functools.partial(sent, pair, k))

    for h in range(heads):
        finish(h)
    collect(last, 0)


def body(queries, grad_out, keys_values, doc_ids):
    layers, rows, width = queries.shape
    kv_width = keys_values.shape[2]
    heads_kv = kv_width // HD
    group = width // kv_width
    n = lax.axis_size("ctx")
    sections = lax.axis_size("section")
    reach = n // 4
    heads = heads_kv // 2
    blocks = reach + 2
    window = (reach + 1) * rows
    piece = rows // sections
    depth = reach // 2
    bf, f32 = jnp.bfloat16, jnp.float32
    dma = pltpu.SemaphoreType.DMA
    hbm = pl.BlockSpec(memory_space=pl.ANY)
    vmem = pl.BlockSpec(memory_space=pltpu.VMEM)
    grad_queries, grad_kv = pl.pallas_call(
        functools.partial(kernel, n, sections, reach, heads_kv, group),
        out_shape=(
            jax.ShapeDtypeStruct((layers * rows, width), bf),
            jax.ShapeDtypeStruct((2, piece, kv_width), bf),
        ),
        in_specs=[hbm, hbm, hbm, hbm],
        out_specs=(hbm, vmem),
        scratch_shapes=[
            pltpu.VMEM((n, rows), jnp.int32),
            pltpu.VMEM((heads, 2, layers * rows, group * HD), bf),
            pltpu.VMEM((heads, 2, layers * rows, group * HD), bf),
            pltpu.VMEM((heads, 2, blocks, rows, HD), bf),
            pltpu.VMEM((2, window, rows), f32),
            pltpu.VMEM((heads, 2, window, group * layers * rows), f32),
            pltpu.VMEM((heads, 2, window, group * layers * rows), f32),
            pltpu.VMEM((heads, 2, depth + 1, 8, group * layers * rows), f32),
            pltpu.VMEM((blocks * rows, 2 * group * layers * rows), bf),
            pltpu.VMEM((heads, blocks * rows, 2 * group * layers * rows), bf),
            pltpu.VMEM((heads, 2, blocks, rows, HD), bf),
            pltpu.VMEM((heads, 2, rows, HD), bf),
            pltpu.VMEM((heads, max(sections - 1, 1), 2, blocks, piece, HD), bf),
            pltpu.VMEM((heads, blocks, 2, piece, HD), bf),
            pltpu.VMEM((depth + 1, 2, heads, 2, piece, HD), bf),
            pltpu.VMEM((heads, 2, layers * rows, group * HD), bf),
            dma,
            dma((heads, 3)),
            dma((heads, 2)),
            dma((heads, 2)),
            dma((heads, depth + 1, 2)),
            dma((heads, blocks)),
            dma((heads,)),
            dma((heads,)),
            dma((heads,)),
            dma((heads,)),
            dma((heads, depth + 1, max(sections - 1, 1), 2)),
            dma((heads, depth + 1, max(sections - 1, 1), 2)),
            dma((heads, blocks, 2)),
            dma((depth + 1, 2, heads, 2)),
            dma((heads,)),
            dma((heads,)),
            dma((heads,)),
        ],
        compiler_params=pltpu.CompilerParams(
            collective_id=0, has_side_effects=True, vmem_limit_bytes=(24 + 4 * reach) * 1024 * 1024
        ),
        name="cross_backward",
    )(
        *[
            pltpu.with_memory_space_constraint(x, pltpu.HBM)
            for x in (
                queries.reshape(layers * rows, width), grad_out.reshape(layers * rows, width),
                keys_values, doc_ids.reshape(n, rows),
            )
        ]
    )
    return grad_queries.reshape(queries.shape), grad_kv


def solution(mesh):
    return jax.shard_map(
        body,
        mesh=mesh,
        in_specs=(P("section", "ctx", None), P("section", "ctx", None), P(None, "ctx", None), P()),
        out_specs=(P("section", "ctx", None), P(None, ("ctx", "section"), None)),
        check_vma=False,
    )
```
